32 devices in a mesh: gx: 8 (over y, x, core), gy: 4 (over z).
Axes of the slice: x: 2, y: 2, z: 4, core: 2. Of those that a mesh axis runs over, the one named last changes fastest.
Arguments:
- dual_distributions: float32 [26, 4, 128, 512], P(None, None, 'gx', 'gy'), may hold values from -6 to 6
- primal_fluid_rho: float32 [4, 128, 512], P(None, 'gx', 'gy'), may hold values from 0.8 to 1.2
- forward_flow_speed: float32 [3, 4, 128, 512], P(None, None, 'gx', 'gy'), may hold values from -0.15 to 0.15
- primal_kelvin_values: float32 [4, 128, 512], P(None, 'gx', 'gy'), may hold values from 0.5 to 1.5
- obstacle_mask: int32 [4, 128, 512], P(None, 'gx', 'gy'), may hold values 0 or 1
- objective_surface_mask: int32 [4, 128, 512], P(None, 'gx', 'gy'), may hold values 0 or 1
- pillar_porosity: float32 [128, 512], P('gx', 'gy'), may hold values from 0 to 1
- pillar_design_patch: int32 [128, 512], P('gx', 'gy'), may hold values from 0 to 15, as said below
- patch_holder: int32 [512, 1], P(('gx', 'gy')), may hold values from 0 to 7; in each aligned block of 16 rows (0 to 15, 16 to 31, ...) at most 4 rows name the same one
Outputs:
- adjoint_next: float32 [26, 4, 128, 512], P(None, None, 'gx', 'gy')
- refreshed_owner_tiles: float32 [1024, 128], P(('gx', 'gy'))
The draws below stay inside these ranges and needn't reach their ends.
Inputs may be any that keep to these rules, and one draw needn't show every extreme that they name: `pillar_design_patch`: on each device, every local block number names exactly 128 of its columns. `patch_holder`: among the 16 blocks of one device, at most 4 have the same owner.
All inputs are finite; a program needn't handle non-finite values. No bound on the sum of `obstacle_mask` or of `objective_surface_mask` on one device may be relied on, other than what follows from the above.
Results may differ from the reference program's by a relative error of at most 0.0003.
Values sent between devices are 32-bit elements; how exact they have to be, the bound alone decides.
A program may use at most 64 MiB of HBM per device.

```python
import math
import jax
import jax.numpy as jnp
import numpy as np
from jax import lax

CX = 16
CY = 128
HEIGHT_PLANES = 4
STEPS = 6
TILE = 128
WIDTH_SITES = 128
BREADTH_SITES = 512
LB = 16
CAP = 4
NBLK = 512
N_GX = 8
N_GY = 4


def draw_pillar_design_patch(key, part):
    keys = jax.random.split(jax.random.fold_in(key, 17), N_GX * N_GY)
    orders = jax.vmap(lambda single: jax.random.permutation(single, CX * CY))(keys)
    labels = (orders // TILE).astype(jnp.int32)
    labels = labels.reshape(N_GX, N_GY, CX, CY).transpose(0, 2, 1, 3)
    return labels.reshape(N_GX * CX, N_GY * CY)


def place_ends(drawn, stream_key, low, top_value):
    longest = drawn.shape.index(max(drawn.shape))
    spots = []
    for shift in (0, 1):
        where = [jax.random.randint(jax.random.fold_in(stream_key, axis), (), 0, length) for axis, length in enumerate(drawn.shape)]
        where[longest] = (where[longest] + shift) % drawn.shape[longest]
        spots.append(tuple(where))
    return drawn.at[spots[0]].set(low).at[spots[1]].set(top_value)


def shard_levels(own_key, dims, cuts, smallest, top_value):
    level, own = 1.0, jax.random.fold_in(own_key, 6)
    for axis_at, shards_of in cuts:
        steps = jnp.exp(jax.random.uniform(jax.random.fold_in(own, axis_at), (shards_of,), jnp.float32, smallest / len(cuts), top_value / len(cuts)))
        level = level * jnp.repeat(steps, dims[axis_at] // shards_of).reshape([-1 if axis == axis_at else 1 for axis in range(len(dims))])
    return level


def routed_block(own_key, own, number, rows, count, top, limit, slope):
    sequence = jax.random.permutation(own_key, count)
    packed, common = load_shares(count, rows * top, limit, slope, True), load_shares(count, rows * top, limit, slope, False)
    places = jnp.arange(count)

    def named(tallies, turn):
        used = int((tallies > 0).sum())
        fixed = max(1, used // 4)
        moved = fixed + (places - fixed + turn * (used - fixed)) % max(1, count - fixed)
        return jnp.zeros((count,), jnp.int32).at[sequence[jnp.where(places < fixed, places, moved)]].set(jnp.asarray(tallies, jnp.int32))

    tallies = jnp.where(number % 4 == 0, named(packed, number // 4), named(common, number - number // 4 - 1))
    mixed = jax.random.permutation(jax.random.fold_in(own, 3), count)
    source_of, taker = mixed[0:count // 2 * 2:2], mixed[1:count // 2 * 2:2]
    room = jnp.minimum(tallies[source_of] - 1, limit - tallies[taker]) // 2
    room = jnp.where((source_of == sequence[0]) | (taker == sequence[0]) | (tallies[taker] == 0), 0, jnp.maximum(room, 0))
    moved = jax.random.randint(jax.random.fold_in(own, 4), (count // 2,), 0, 1 << 20) % (room + 1)
    tallies = tallies.at[source_of].add(-moved).at[taker].add(moved)
    items = jnp.searchsorted(jnp.cumsum(tallies), jnp.arange(rows * top), side="right").astype(jnp.int32)
    listing = items.reshape(top, rows).T
    listing = listing[jax.random.permutation(jax.random.fold_in(own, 1), rows)]
    turn = jax.random.randint(jax.random.fold_in(own, 2), (rows, 1), 0, top)
    return jnp.take_along_axis(listing, (jnp.arange(top)[None, :] + turn) % top, axis=1)


def load_shares(count, total, bound, lean, full):
    portions = [(1 << 20) // math.isqrt(grade ** lean) + 1 for grade in range(1, count + 1)]
    largest = bound if full else min(bound, max(-(-total // count), total * portions[0] // sum(portions)))
    least = 1 if total - largest >= count - 1 else 0
    given, surplus = [largest] + [least] * (count - 1), total - largest - least * (count - 1)
    while surplus > 0:
        candidates = [i for i in range(1, count) if given[i] < largest] or [i for i in range(1, count) if given[i] < bound]
        mass, remaining = sum([portions[i] for i in candidates]), surplus
        for i in candidates:
            more = min(bound - given[i], max(1, remaining * portions[i] // mass), surplus)
            given[i] = given[i] + more
            surplus = surplus - more
    return np.array(given)


def gaussian(own_key, shape, deviation, limit, cuts=(), kind=jnp.bfloat16):
    gain = shard_levels(own_key, shape, cuts, -0.22, 0.18) if cuts else 1.0
    array = jax.random.normal(own_key, shape, jnp.float32) * deviation * gain
    return jnp.minimum(jnp.maximum(array, -limit), limit).astype(kind)


def setup_inputs(seed: int = 0) -> dict:
    key_list = jax.random.split(jax.random.key(seed), 10)
    dual_distributions = gaussian(key_list[0], (26, HEIGHT_PLANES, WIDTH_SITES, BREADTH_SITES), 1.0, 6.0, ((2, 8), (3, 4)), jnp.float32)
    primal_fluid_rho = jnp.clip(0.8 + 0.40000004 * jax.random.uniform(key_list[1], (HEIGHT_PLANES, WIDTH_SITES, BREADTH_SITES), jnp.float32) ** shard_levels(key_list[1], (HEIGHT_PLANES, WIDTH_SITES, BREADTH_SITES), ((1, 8), (2, 4)), -0.2, 0.2), 0.8, 1.2)
    forward_flow_speed = jnp.clip(jax.random.uniform(key_list[2], (3, HEIGHT_PLANES, WIDTH_SITES, BREADTH_SITES), jnp.float32, -0.15, 0.15) * shard_levels(key_list[2], (3, HEIGHT_PLANES, WIDTH_SITES, BREADTH_SITES), ((2, 8), (3, 4)), -0.4, 0.0), -0.15, 0.15)
    primal_kelvin_values = jnp.clip(0.5 + 1.0 * jax.random.uniform(key_list[3], (HEIGHT_PLANES, WIDTH_SITES, BREADTH_SITES), jnp.float32) ** shard_levels(key_list[3], (HEIGHT_PLANES, WIDTH_SITES, BREADTH_SITES), ((1, 8), (2, 4)), -0.2, 0.2), 0.5, 1.5)
    obstacle_mask = place_ends((jax.random.randint(key_list[4], (HEIGHT_PLANES, WIDTH_SITES, BREADTH_SITES), 0, 10) < 3).astype(jnp.int32), jax.random.fold_in(key_list[4], 1), 0, 1)
    objective_surface_mask = place_ends((jax.random.randint(key_list[5], (HEIGHT_PLANES, WIDTH_SITES, BREADTH_SITES), 0, 8) < 1).astype(jnp.int32), jax.random.fold_in(key_list[5], 1), 0, 1)
    pillar_porosity = jnp.clip(1.0 * jax.random.uniform(key_list[6], (WIDTH_SITES, BREADTH_SITES), jnp.float32) ** shard_levels(key_list[6], (WIDTH_SITES, BREADTH_SITES), ((0, 8), (1, 4)), -0.2, 0.2), 0.0, 1.0)
    pillar_design_patch = draw_pillar_design_patch(jax.random.fold_in(key_list[9], 71), 0)
    patch_holder_keys = jax.random.split(jax.random.fold_in(key_list[8], 1), NBLK // LB)
    patch_holder_turns = jax.random.permutation(jax.random.fold_in(key_list[8], 3), NBLK // LB)
    patch_holder = jax.vmap(lambda own, number: routed_block(jax.random.fold_in(key_list[8], 2), own, number, LB, N_GX, 1, CAP, 2))(patch_holder_keys, patch_holder_turns).reshape((NBLK, 1))
    return {"dual_distributions": dual_distributions, "primal_fluid_rho": primal_fluid_rho, "forward_flow_speed": forward_flow_speed, "primal_kelvin_values": primal_kelvin_values, "obstacle_mask": obstacle_mask, "objective_surface_mask": objective_surface_mask, "pillar_porosity": pillar_porosity, "pillar_design_patch": pillar_design_patch, "patch_holder": patch_holder}


VELOCITIES = ((0, 0, 0), (1, 0, 0), (-1, 0, 0), (0, 1, 0), (0, -1, 0), (0, 0, 1), (0, 0, -1), (1, 1, 0), (-1, -1, 0), (1, -1, 0), (-1, 1, 0), (1, 0, 1), (-1, 0, -1), (1, 0, -1), (-1, 0, 1), (0, 1, 1), (0, -1, -1), (0, 1, -1), (0, -1, 1))
FLOW_WEIGHTS = (1.0 / 3.0,) + (1.0 / 18.0,) * 6 + (1.0 / 36.0,) * 12
HEAT_WEIGHTS = (0.25,) + (0.125,) * 6
OMEGA_FLOW = 1.6
CONDUCT_RATE = 1.2
SOURCE_RATE = 0.5
HEAT_RATE = 0.1
STEP_SIZE = 0.1

def opposite(count_total):
    if count_total == 0:
        return 0
    return count_total + 1 if count_total % 2 == 1 else count_total - 1

def build_grid_setup(primal_fluid_rho, forward_flow_speed, primal_kelvin_values, obstacle_mask, objective_surface_mask):
    fluid_part = 1.0 - obstacle_mask.astype(jnp.float32)
    advected_warmness_term = 4.0 * CONDUCT_RATE * primal_kelvin_values / primal_fluid_rho
    sender_rank = SOURCE_RATE * objective_surface_mask.astype(jnp.float32)
    return jnp.stack([primal_fluid_rho, forward_flow_speed[0] * fluid_part, forward_flow_speed[1] * fluid_part, forward_flow_speed[2] * fluid_part, advected_warmness_term, fluid_part, sender_rank])

def propagate(padded):
    center = padded[:, :, 1:-1, 1:-1]
    extent_x = padded.shape[2] - 2
    extent_y = padded.shape[3] - 2
    fetched_neighbours = []
    for count_total in range(26):
        within = count_total if count_total < 19 else count_total - 19
        offset = 0 if count_total < 19 else 19
        step_x, step_y, step_z = VELOCITIES[within]
        shifted = padded[count_total, :, 1 + step_x:1 + step_x + extent_x, 1 + step_y:1 + step_y + extent_y]
        reflected = center[offset + opposite(within)]
        if step_z == 1:
            shifted = jnp.concatenate([shifted[1:], reflected[-1:]], axis=0)
        elif step_z == -1:
            shifted = jnp.concatenate([reflected[:1], shifted[:-1]], axis=0)
        fetched_neighbours.append(shifted)
    return fetched_neighbours

def dotted(direction, parts):
    result = 0.0
    for component in range(3):
        if direction[component] != 0:
            result = result + float(direction[component]) * parts[component]
    return result

def collide(fetched_neighbours, constant_arguments):
    primal_fluid_rho = constant_arguments[0]
    forward_flow_speed = [constant_arguments[1], constant_arguments[2], constant_arguments[3]]
    advected_warmness_term = constant_arguments[4]
    fluid_part = constant_arguments[5]
    sender_rank = constant_arguments[6]
    speed_sq = forward_flow_speed[0] * forward_flow_speed[0] + forward_flow_speed[1] * forward_flow_speed[1] + forward_flow_speed[2] * forward_flow_speed[2]
    scalar = 0.0
    vector = [0.0, 0.0, 0.0]
    for count_total in range(19):
        direction = VELOCITIES[count_total]
        projected = dotted(direction, forward_flow_speed)
        weighted = FLOW_WEIGHTS[count_total] * fetched_neighbours[count_total]
        scalar = scalar + weighted * (1.0 + 4.5 * projected * projected - 1.5 * speed_sq)
        for component in range(3):
            if direction[component] != 0:
                vector[component] = vector[component] + 3.0 * direction[component] * weighted
    ambient_kelvin_level = 0.0
    heat_vec = [0.0, 0.0, 0.0]
    heat_sum = 0.0
    for count_total in range(7):
        direction = VELOCITIES[count_total]
        weighted = HEAT_WEIGHTS[count_total] * fetched_neighbours[19 + count_total]
        ambient_kelvin_level = ambient_kelvin_level + weighted * (1.0 + 4.0 * dotted(direction, forward_flow_speed))
        heat_sum = heat_sum + weighted
        for component in range(3):
            if direction[component] != 0:
                heat_vec[component] = heat_vec[component] + float(direction[component]) * weighted
    heat_drift = heat_vec[0] * forward_flow_speed[0] + heat_vec[1] * forward_flow_speed[1] + heat_vec[2] * forward_flow_speed[2]
    refreshed_owner_tiles = []
    for count_total in range(19):
        direction = VELOCITIES[count_total]
        relaxed = (1.0 - OMEGA_FLOW) * fetched_neighbours[count_total] + OMEGA_FLOW * (scalar + dotted(direction, vector)) + advected_warmness_term * (dotted(direction, heat_vec) - heat_drift)
        refreshed_owner_tiles.append(fluid_part * relaxed + (1.0 - fluid_part) * fetched_neighbours[opposite(count_total)])
    for count_total in range(7):
        refreshed_owner_tiles.append((1.0 - CONDUCT_RATE) * fetched_neighbours[19 + count_total] + CONDUCT_RATE * ambient_kelvin_level + sender_rank)
    sens = -primal_fluid_rho * (forward_flow_speed[0] * vector[0] + forward_flow_speed[1] * vector[1] + forward_flow_speed[2] * vector[2]) + HEAT_RATE * heat_sum
    return (jnp.stack(refreshed_owner_tiles), sens)

def placement(owners, groups, capacity):
    hits = (owners[..., None] == jnp.arange(groups, dtype=jnp.int32)).astype(jnp.int32)
    rank = lax.optimization_barrier(jnp.sum((jnp.cumsum(hits, axis=-2) - hits) * hits, axis=-1))
    slot = owners * capacity + rank
    return (slot[..., None] == jnp.arange(groups * capacity, dtype=jnp.int32)).astype(jnp.float32)

def renew(received):
    sens = received[..., 0, :]
    current = received[..., 1, :]
    spread = jnp.sqrt(lax.optimization_barrier(jnp.mean(sens * sens, axis=-1, keepdims=True)) + 1e-06)
    return jnp.clip(current - STEP_SIZE * sens / spread, 0.0, 1.0)

def arrange(field):
    return field.reshape(N_GX, CX, N_GY, CY).transpose(0, 2, 1, 3).reshape(N_GX * N_GY, CX * CY)

def reference(dual_distributions, primal_fluid_rho, forward_flow_speed, primal_kelvin_values, obstacle_mask, objective_surface_mask, pillar_porosity, pillar_design_patch, patch_holder):
    constant_arguments = build_grid_setup(primal_fluid_rho, forward_flow_speed, primal_kelvin_values, obstacle_mask, objective_surface_mask)
    state = dual_distributions
    total = jnp.zeros(primal_fluid_rho.shape, jnp.float32)
    for step in range(STEPS):
        padded = jnp.pad(state, ((0, 0), (0, 0), (1, 1), (1, 1)))
        state, sens = collide(propagate(padded), constant_arguments)
        total = total + sens
    column = lax.optimization_barrier(jnp.sum(total, axis=0))
    symmetric = column + column[::-1, :] + column[:, ::-1] + column[::-1, ::-1]
    order = jnp.argsort(arrange(pillar_design_patch), axis=1, stable=True)
    devices = N_GX * N_GY
    sens_tiles = jnp.take_along_axis(arrange(symmetric), order, 1).reshape(devices, LB, TILE)
    design_tiles = jnp.take_along_axis(arrange(pillar_porosity), order, 1).reshape(devices, LB, TILE)
    tiles = jnp.stack([sens_tiles, design_tiles], axis=2).reshape(devices, LB, 2 * TILE)
    place = placement(patch_holder.reshape(devices, LB), N_GX, CAP)
    outgoing = jnp.einsum('dls,dlt->dst', place, tiles, precision=lax.Precision.HIGHEST)
    outgoing = outgoing.reshape(N_GX, N_GY, N_GX, CAP, 2, TILE).transpose(2, 1, 0, 3, 4, 5)
    refreshed_owner_tiles = renew(outgoing)
    return (state, refreshed_owner_tiles.reshape(N_GX * N_GY * N_GX * CAP, TILE))
```

```python
import functools

import jax
import jax.numpy as jnp
from jax import lax
from jax.experimental import pallas as pl
from jax.experimental.pallas import tpu as pltpu
from jax.sharding import PartitionSpec as P

STEPS = 6
TILE = 128

VELOCITIES = (
    (0, 0, 0),
    (1, 0, 0),
    (-1, 0, 0),
    (0, 1, 0),
    (0, -1, 0),
    (0, 0, 1),
    (0, 0, -1),
    (1, 1, 0),
    (-1, -1, 0),
    (1, -1, 0),
    (-1, 1, 0),
    (1, 0, 1),
    (-1, 0, -1),
    (1, 0, -1),
    (-1, 0, 1),
    (0, 1, 1),
    (0, -1, -1),
    (0, 1, -1),
    (0, -1, 1),
)
W0, W1, W2 = 1.0 / 3.0, 1.0 / 18.0, 1.0 / 36.0
V0, V1 = 0.25, 0.125
FLOW = 19
POPS = 26
OMEGA_FLOW = 1.6
CONDUCT_RATE = 1.2
SOURCE_RATE = 0.5
HEAT_RATE = 0.1
STEP_SIZE = 0.1

DIRS = ((-1, 0), (1, 0), (0, -1), (0, 1), (-1, -1), (1, -1), (-1, 1), (1, 1))
MESH = pl.DeviceIdType.MESH
PAD = 8


def velocity(pop):
    return VELOCITIES[pop if pop < FLOW else pop - FLOW]


def opposite(pop):
    base = 0 if pop < FLOW else FLOW
    within = pop - base
    if within == 0:
        return pop
    return base + (within + 1 if within % 2 == 1 else within - 1)


def moving(axis, sign):
    return [pop for pop in range(POPS) if velocity(pop)[axis] == sign]


XPOPS = (moving(0, 1), moving(0, -1))
YPOPS = (moving(1, 1), moving(1, -1))


def split3(value):
    high = value.astype(jnp.bfloat16)
    rest = value - high.astype(jnp.float32)
    middle = rest.astype(jnp.bfloat16)
    low = (rest - middle.astype(jnp.float32)).astype(jnp.bfloat16)
    return high, middle, low


def body(
    sizes,
    f_hbm,
    rho_ref,
    speed_ref,
    kelvin_ref,
    obstacle_ref,
    surface_ref,
    porosity_ref,
    patch_ref,
    holder_ref,
    out_hbm,
    tiles_ref,
    state,
    const,
    acc,
    xsend,
    xrecv,
    ysend,
    yrecv,
    csend,
    crecv,
    yhalo,
    hot,
    label_rows,
    flip_a,
    flip_b,
    column,
    mirror,
    outgoing,
    received,
    load_sem,
    store_sem,
    send_sem,
    recv_sem,
    msend_sem,
    mrecv_sem,
    asend_sem,
    arecv_sem,
):
    nx, ny, height, ex, ey, blocks, cap = sizes
    i = lax.axis_index("gx")
    j = lax.axis_index("gy")
    tiles_of = ex // 8

    load = pltpu.make_async_copy(f_hbm, state.at[0, :, :, pl.ds(PAD, ex), :], load_sem)
    load.start()

    barrier = pltpu.get_barrier_semaphore()

    def inside(di, dj):
        a, b = i + di, j + dj
        return (a >= 0) & (a < nx) & (b >= 0) & (b < ny)

    xrecv[...] = jnp.zeros(xrecv.shape, jnp.float32)
    yrecv[...] = jnp.zeros(yrecv.shape, jnp.float32)
    crecv[...] = jnp.zeros(crecv.shape, jnp.float32)
    acc[...] = jnp.zeros(acc.shape, jnp.float32)

    mirrors = ((nx - 1 - i, j), (i, ny - 1 - j), (nx - 1 - i, ny - 1 - j))
    for dx, dy in DIRS:
        @pl.when(inside(dx, dy))
        def _():
            pl.semaphore_signal(barrier, inc=1, device_id=(i + dx, j + dy), device_id_type=MESH)
    for d in range(1, nx):
        pl.semaphore_signal(barrier, inc=1, device_id=(lax.rem(i + d, nx), j), device_id_type=MESH)
    for target in mirrors:
        pl.semaphore_signal(barrier, inc=1, device_id=target, device_id_type=MESH)

    lane = lax.broadcasted_iota(jnp.int32, (8, ey), 1)

    for z in range(height):
        fluid = 1.0 - obstacle_ref[z].astype(jnp.float32)
        for axis in range(3):
            const[axis, z] = speed_ref[axis, z] * fluid
        const[3, z] = 4.0 * CONDUCT_RATE * kelvin_ref[z] / rho_ref[z]
        const[4, z] = SOURCE_RATE * surface_ref[z].astype(jnp.float32)
        const[5, z] = fluid

    wide = 1 + (i > 0).astype(jnp.int32) + (i < nx - 1).astype(jnp.int32)
    deep = 1 + (j > 0).astype(jnp.int32) + (j < ny - 1).astype(jnp.int32)
    pl.semaphore_wait(barrier, wide * deep - 1 + nx - 1 + len(mirrors))
    load.wait()

    def rim_copy(par, k):
        dx, dy = DIRS[k]
        if k < 2:
            src, dst = xsend.at[par, k], xrecv.at[par, k]
        elif k < 4:
            src, dst = ysend.at[par, k - 2], yrecv.at[par, k - 2]
        else:
            src, dst = csend.at[par, k - 4], crecv.at[par, k - 4]
        return pltpu.make_async_remote_copy(
            src_ref=src,
            dst_ref=dst,
            send_sem=send_sem.at[par, k],
            recv_sem=recv_sem.at[par, k],
            device_id=(i + dx, j + dy),
            device_id_type=MESH,
        )

    def send_rim(par):
        for side in range(2):
            row = PAD if side == 0 else PAD + ex - 1
            for p, pop in enumerate(XPOPS[side]):
                for z in range(height):
                    q = p * height + z
                    xsend[par, side, q : q + 1, :] = state[par, pop, z, row : row + 1, :]
        for k in range(2):
            @pl.when(inside(*DIRS[k]))
            def _():
                rim_copy(par, k).start()
        for side in range(2):
            for rt in range(tiles_of):
                packed = jnp.zeros((8, ey), jnp.float32)
                for p, pop in enumerate(YPOPS[side]):
                    for z in range(height):
                        q = p * height + z
                        value = state[par, pop, z, PAD + rt * 8 : PAD + rt * 8 + 8, :]
                        shift = q if side == 0 else (q + 1) % ey
                        if shift:
                            value = pltpu.roll(value, shift, 1)
                        packed = jnp.where(lane == q, value, packed)
                ysend[par, side, rt * 8 : rt * 8 + 8, :] = packed
                for k in range(4, 8):
                    dx, dy = DIRS[k]
                    if (0 if dy < 0 else 1) == side:
                        if dx < 0 and rt == 0:
                            csend[par, k - 4] = packed[0:1, :]
                        if dx > 0 and rt == tiles_of - 1:
                            csend[par, k - 4] = packed[7:8, :]
        for k in range(4, 8):
            @pl.when(inside(*DIRS[k]))
            def _():
                rim_copy(par, k).start()
        for k in range(2, 4):
            @pl.when(inside(*DIRS[k]))
            def _():
                rim_copy(par, k).start()

    def take_rim(par):
        for k in range(8):
            dx, dy = DIRS[k]

            @pl.when(inside(dx, dy))
            def _():
                rim_copy(par, k).wait_send()

            @pl.when(inside(-dx, -dy))
            def _():
                rim_copy(par, k).wait_recv()
        for side in range(2):
            row = PAD + ex if side == 0 else PAD - 1
            for p, pop in enumerate(XPOPS[side]):
                for z in range(height):
                    q = p * height + z
                    state[par, pop, z, row : row + 1, :] = xrecv[par, side, q : q + 1, :]
            yhalo[side, PAD : PAD + ex, :] = yrecv[par, side]
        for k in range(4, 8):
            dx, dy = DIRS[k]
            row = PAD + ex if dx < 0 else PAD - 1
            yhalo[0 if dy < 0 else 1, row : row + 1, :] = crecv[par, k - 4]

    def collide(par, z, rt):
        start = PAD + rt * 8

        def pull(pop):
            cx, cy, cz = velocity(pop)
            zz = z + cz
            if zz < 0 or zz >= height:
                return state[par, opposite(pop), z, start : start + 8, :]
            value = state[par, pop, zz, start + cx : start + cx + 8, :]
            if cy:
                side = 0 if cy == 1 else 1
                q = YPOPS[side].index(pop) * height + zz
                edge = yhalo[side, start + cx : start + cx + 8, :]
                last = ey - 1 if cy == 1 else 0
                shift = (last - q) % ey
                if shift:
                    edge = pltpu.roll(edge, shift, 1)
                value = pltpu.roll(value, (-cy) % ey, 1)
                value = jnp.where(lane == last, edge, value)
            return value

        rows = slice(rt * 8, rt * 8 + 8)
        ux, uy, uz = const[0, z, rows, :], const[1, z, rows, :], const[2, z, rows, :]
        coupling = const[3, z, rows, :]
        source = const[4, z, rows, :]
        fluid = const[5, z, rows, :] > 0.5

        b = [pull(FLOW + k) for k in range(7)]
        tsum = V0 * b[0] + V1 * ((b[1] + b[2]) + (b[3] + b[4]) + (b[5] + b[6]))
        qx, qy, qz = V1 * (b[1] - b[2]), V1 * (b[3] - b[4]), V1 * (b[5] - b[6])
        qu = qx * ux + qy * uy + qz * uz
        warm = CONDUCT_RATE * (tsum + 4.0 * qu) + source
        for k in range(7):
            state[1 - par, FLOW + k, z, start : start + 8, :] = (1.0 - CONDUCT_RATE) * b[k] + warm

        a = [pull(k) for k in range(FLOW)]
        sm = {k: a[k] + a[k + 1] for k in range(1, FLOW, 2)}
        df = {k: a[k] - a[k + 1] for k in range(1, FLOW, 2)}
        sx = (3.0 * W1) * df[1] + (3.0 * W2) * ((df[7] + df[9]) + (df[11] + df[13]))
        sy = (3.0 * W1) * df[3] + (3.0 * W2) * ((df[7] - df[9]) + (df[15] + df[17]))
        sz = (3.0 * W1) * df[5] + (3.0 * W2) * ((df[11] - df[13]) + (df[15] - df[17]))
        xy, xz, yz = sm[7] + sm[9], sm[11] + sm[13], sm[15] + sm[17]
        mass = W0 * a[0] + W1 * (sm[1] + sm[3] + sm[5]) + W2 * (xy + xz + yz)
        quad = (
            (ux * ux) * (W1 * sm[1] + W2 * (xy + xz))
            + (uy * uy) * (W1 * sm[3] + W2 * (xy + yz))
            + (uz * uz) * (W1 * sm[5] + W2 * (xz + yz))
            + (2.0 * W2)
            * (
                (ux * uy) * (sm[7] - sm[9])
                + (ux * uz) * (sm[11] - sm[13])
                + (uy * uz) * (sm[15] - sm[17])
            )
        )
        square = ux * ux + uy * uy + uz * uz
        scalar = mass * (1.0 - 1.5 * square) + 4.5 * quad
        base = OMEGA_FLOW * scalar - coupling * qu
        gx = OMEGA_FLOW * sx + coupling * qx
        gy = OMEGA_FLOW * sy + coupling * qy
        gz = OMEGA_FLOW * sz + coupling * qz
        along = {
            1: gx,
            3: gy,
            5: gz,
            7: gx + gy,
            9: gx - gy,
            11: gx + gz,
            13: gx - gz,
            15: gy + gz,
            17: gy - gz,
        }
        keep = 1.0 - OMEGA_FLOW

        def put(pop, value):
            state[1 - par, pop, z, start : start + 8, :] = value

        put(0, jnp.where(fluid, keep * a[0] + base, a[0]))
        for k in range(1, FLOW, 2):
            put(k, jnp.where(fluid, keep * a[k] + (base + along[k]), a[k + 1]))
            put(k + 1, jnp.where(fluid, keep * a[k + 1] + (base - along[k]), a[k]))
        return HEAT_RATE * tsum - rho_ref[z, rows, :] * (ux * sx + uy * sy + uz * sz)

    send_rim(0)

    number = lax.broadcasted_iota(jnp.int32, (blocks, ey), 0)
    below = (
        lax.broadcasted_iota(jnp.int32, (ey, ey), 0) < lax.broadcasted_iota(jnp.int32, (ey, ey), 1)
    ).astype(jnp.bfloat16)
    place = lax.broadcasted_iota(jnp.int32, (TILE, ey), 0).astype(jnp.float32)
    running = jnp.zeros((blocks, 1), jnp.float32)
    for x in range(ex):
        hits = (patch_ref[x : x + 1, :] == number).astype(jnp.float32)
        earlier = jnp.dot(
            hits.astype(jnp.bfloat16), below, preferred_element_type=jnp.float32
        )
        rank = jnp.sum(hits * (earlier + running), axis=0, keepdims=True)
        running = running + jnp.sum(hits, axis=1, keepdims=True)
        hot[:, x * ey : (x + 1) * ey] = (place == rank).astype(jnp.bfloat16)
        label_rows[:, x * ey : (x + 1) * ey] = hits

    def gathered(field):
        columns = jnp.concatenate(
            [
                label_rows[:, x * ey : (x + 1) * ey] * field[x : x + 1, :]
                for x in range(ex)
            ],
            axis=1,
        )
        parts = jnp.concatenate(split3(columns), axis=0)
        result = lax.dot_general(
            parts, hot[...], (((1,), (1,)), ((), ())), preferred_element_type=jnp.float32
        )
        return result[:blocks] + result[blocks : 2 * blocks] + result[2 * blocks :]

    design = gathered(porosity_ref[...])

    owner = jnp.broadcast_to(holder_ref[...], (blocks, TILE)).astype(jnp.float32)
    rows_of = lax.broadcasted_iota(jnp.int32, (blocks, TILE), 0)
    lanes_of = lax.broadcasted_iota(jnp.int32, (blocks, TILE), 1)
    diagonal = (rows_of == lanes_of).astype(jnp.float32)
    owner_row = jnp.sum(owner * diagonal, axis=0, keepdims=True)
    same = ((owner == owner_row) & (rows_of < lanes_of) & (lanes_of < blocks)).astype(jnp.float32)
    rank_row = jnp.sum(same, axis=0, keepdims=True)
    slot_row = owner_row * float(cap) + rank_row
    slots = nx * cap
    choose = (
        (lax.broadcasted_iota(jnp.int32, (slots, TILE), 0).astype(jnp.float32) == slot_row)
        & (lax.broadcasted_iota(jnp.int32, (slots, TILE), 1) < blocks)
    ).astype(jnp.bfloat16)

    def step(s, carry):
        par = lax.rem(s, 2)
        take_rim(par)
        for rt in range(tiles_of):
            sens = collide(par, 0, rt)
            for z in range(1, height):
                sens = sens + collide(par, z, rt)
            acc[rt * 8 : rt * 8 + 8, :] += sens

        @pl.when(s < STEPS - 1)
        def _():
            send_rim(1 - par)

        return carry

    lax.fori_loop(0, STEPS, step, 0)

    last = STEPS % 2
    store = pltpu.make_async_copy(state.at[last, :, :, pl.ds(PAD, ex), :], out_hbm, store_sem)
    store.start()

    column[...] = acc[...]

    def mirror_copy(m):
        return pltpu.make_async_remote_copy(
            src_ref=column,
            dst_ref=mirror.at[m],
            send_sem=msend_sem.at[m],
            recv_sem=mrecv_sem.at[m],
            device_id=mirrors[m],
            device_id_type=MESH,
        )

    for m in (2, 1, 0):
        mirror_copy(m).start()
    for m in range(3):
        mirror_copy(m).wait()
    for x in range(ex):
        flip_a[x : x + 1, :] = mirror[0, ex - 1 - x : ex - x, :]
        flip_b[x : x + 1, :] = mirror[2, ex - 1 - x : ex - x, :]
    reverse = (
        lax.broadcasted_iota(jnp.int32, (ey, ey), 0) + lax.broadcasted_iota(jnp.int32, (ey, ey), 1)
        == ey - 1
    ).astype(jnp.bfloat16)
    turned = jnp.dot(
        jnp.concatenate(split3(mirror[1] + flip_b[...]), axis=0),
        reverse,
        preferred_element_type=jnp.float32,
    )
    symmetric = (
        column[...] + flip_a[...] + (turned[:ex] + turned[ex : 2 * ex] + turned[2 * ex :])
    )
    sens = gathered(symmetric)
    spread = jnp.sqrt(jnp.mean(sens * sens, axis=1, keepdims=True) + 1e-06)
    fresh = jnp.clip(design - STEP_SIZE * sens / spread, 0.0, 1.0)
    padded = jnp.concatenate([fresh, jnp.zeros((TILE - blocks, TILE), jnp.float32)], axis=0)
    parts = jnp.concatenate(split3(padded), axis=1)
    sent = jnp.dot(choose, parts, preferred_element_type=jnp.float32)
    sent = sent[:, :TILE] + sent[:, TILE : 2 * TILE] + sent[:, 2 * TILE :]
    for o in range(nx):
        outgoing[o] = sent[o * cap : (o + 1) * cap, :]

    def owner_copy(d):
        target = lax.rem(i + d, nx)
        return pltpu.make_async_remote_copy(
            src_ref=outgoing.at[target],
            dst_ref=received.at[i],
            send_sem=asend_sem.at[d],
            recv_sem=arecv_sem.at[d],
            device_id=(target, j),
            device_id_type=MESH,
        )

    def arriving(d):
        origin = lax.rem(i + nx - d, nx)
        return pltpu.make_async_remote_copy(
            src_ref=outgoing.at[origin],
            dst_ref=received.at[origin],
            send_sem=asend_sem.at[d],
            recv_sem=arecv_sem.at[d],
            device_id=(origin, j),
            device_id_type=MESH,
        )

    for d in range(1, nx):
        owner_copy(d).start()
    received[i] = outgoing[i]
    for d in range(1, nx):
        owner_copy(d).wait_send()
        arriving(d).wait_recv()
    for o in range(nx):
        tiles_ref[o * cap : (o + 1) * cap, :] = received[o]
    store.wait()


def on_device(
    dual_distributions,
    primal_fluid_rho,
    forward_flow_speed,
    primal_kelvin_values,
    obstacle_mask,
    objective_surface_mask,
    pillar_porosity,
    pillar_design_patch,
    patch_holder,
):
    nx, ny = lax.axis_size("gx"), lax.axis_size("gy")
    pops, height, ex, ey = dual_distributions.shape
    blocks = ex * ey // TILE
    cap = max(2, 2 * blocks // nx)
    nxp, nyp = len(XPOPS[0]), len(YPOPS[0])
    f32 = jnp.float32
    vmem = pl.BlockSpec(memory_space=pltpu.VMEM)
    hbm = pl.BlockSpec(memory_space=pl.ANY)
    return pl.pallas_call(
        functools.partial(body, (nx, ny, height, ex, ey, blocks, cap)),
        out_shape=(
            jax.ShapeDtypeStruct(dual_distributions.shape, f32),
            jax.ShapeDtypeStruct((nx * cap, TILE), f32),
        ),
        in_specs=[hbm] + [vmem] * 8,
        out_specs=(hbm, vmem),
        scratch_shapes=[
            pltpu.VMEM((2, pops, height, ex + 2 * PAD, ey), f32),
            pltpu.VMEM((6, height, ex, ey), f32),
            pltpu.VMEM((ex, ey), f32),
            pltpu.VMEM((2, 2, nxp * height, ey), f32),
            pltpu.VMEM((2, 2, nxp * height, ey), f32),
            pltpu.VMEM((2, 2, ex, ey), f32),
            pltpu.VMEM((2, 2, ex, ey), f32),
            pltpu.VMEM((2, 4, 1, ey), f32),
            pltpu.VMEM((2, 4, 1, ey), f32),
            pltpu.VMEM((2, ex + 2 * PAD, ey), f32),
            pltpu.VMEM((TILE, ex * ey), jnp.bfloat16),
            pltpu.VMEM((blocks, ex * ey), f32),
            pltpu.VMEM((ex, ey), f32),
            pltpu.VMEM((ex, ey), f32),
            pltpu.VMEM((ex, ey), f32),
            pltpu.VMEM((3, ex, ey), f32),
            pltpu.VMEM((nx, cap, TILE), f32),
            pltpu.VMEM((nx, cap, TILE), f32),
            pltpu.SemaphoreType.DMA,
            pltpu.SemaphoreType.DMA,
            pltpu.SemaphoreType.DMA((2, 8)),
            pltpu.SemaphoreType.DMA((2, 8)),
            pltpu.SemaphoreType.DMA((3,)),
            pltpu.SemaphoreType.DMA((3,)),
            pltpu.SemaphoreType.DMA((nx,)),
            pltpu.SemaphoreType.DMA((nx,)),
        ],
        compiler_params=pltpu.CompilerParams(collective_id=0, has_side_effects=True),
    )(
        dual_distributions,
        primal_fluid_rho,
        forward_flow_speed,
        primal_kelvin_values,
        obstacle_mask,
        objective_surface_mask,
        pillar_porosity,
        pillar_design_patch,
        patch_holder,
    )


def solution(mesh):
    in_specs = (
        P(None, None, "gx", "gy"),
        P(None, "gx", "gy"),
        P(None, None, "gx", "gy"),
        P(None, "gx", "gy"),
        P(None, "gx", "gy"),
        P(None, "gx", "gy"),
        P("gx", "gy"),
        P("gx", "gy"),
        P(("gx", "gy"), None),
    )
    out_specs = (P(None, None, "gx", "gy"), P(("gx", "gy"), None))
    return jax.shard_map(
        on_device, mesh=mesh, in_specs=in_specs, out_specs=out_specs, check_vma=False
    )
```

```python
import functools

import jax
import jax.numpy as jnp
from jax import lax
from jax.experimental import pallas as pl
from jax.experimental.pallas import tpu as pltpu
from jax.sharding import PartitionSpec as P

STEPS = 6
TILE = 128

VELOCITIES = (
    (0, 0, 0),
    (1, 0, 0),
    (-1, 0, 0),
    (0, 1, 0),
    (0, -1, 0),
    (0, 0, 1),
    (0, 0, -1),
    (1, 1, 0),
    (-1, -1, 0),
    (1, -1, 0),
    (-1, 1, 0),
    (1, 0, 1),
    (-1, 0, -1),
    (1, 0, -1),
    (-1, 0, 1),
    (0, 1, 1),
    (0, -1, -1),
    (0, 1, -1),
    (0, -1, 1),
)
W0, W1, W2 = 1.0 / 3.0, 1.0 / 18.0, 1.0 / 36.0
V0, V1 = 0.25, 0.125
FLOW = 19
POPS = 26
OMEGA_FLOW = 1.6
CONDUCT_RATE = 1.2
SOURCE_RATE = 0.5
HEAT_RATE = 0.1
STEP_SIZE = 0.1

DIRS = ((-1, 0), (1, 0), (0, -1), (0, 1), (-1, -1), (1, -1), (-1, 1), (1, 1))
MESH = pl.DeviceIdType.MESH
PAD = 8


def velocity(pop):
    return VELOCITIES[pop if pop < FLOW else pop - FLOW]


def opposite(pop):
    base = 0 if pop < FLOW else FLOW
    within = pop - base
    if within == 0:
        return pop
    return base + (within + 1 if within % 2 == 1 else within - 1)


def moving(axis, sign):
    return [pop for pop in range(POPS) if velocity(pop)[axis] == sign]


XPOPS = (moving(0, 1), moving(0, -1))
YPOPS = (moving(1, 1), moving(1, -1))


def split3(value):
    high = value.astype(jnp.bfloat16)
    rest = value - high.astype(jnp.float32)
    middle = rest.astype(jnp.bfloat16)
    low = (rest - middle.astype(jnp.float32)).astype(jnp.bfloat16)
    return high, middle, low


def body(
    sizes,
    f_hbm,
    rho_hbm,
    speed_hbm,
    kelvin_hbm,
    obstacle_hbm,
    surface_hbm,
    porosity_hbm,
    patch_hbm,
    holder_hbm,
    out_hbm,
    tiles_ref,
    rho_ref,
    speed_ref,
    kelvin_ref,
    obstacle_ref,
    surface_ref,
    porosity_ref,
    patch_ref,
    holder_ref,
    state,
    const,
    acc,
    xsend,
    xrecv,
    ysend,
    yrecv,
    csend,
    crecv,
    yhalo,
    hot,
    label_rows,
    flip_a,
    flip_b,
    column,
    mirror,
    outgoing,
    received,
    load_sem,
    store_sem,
    send_sem,
    recv_sem,
    msend_sem,
    mrecv_sem,
    asend_sem,
    arecv_sem,
):
    nx, ny, height, ex, ey, blocks, cap = sizes
    i = lax.axis_index("gx")
    j = lax.axis_index("gy")
    tiles_of = ex // 8

    load = pltpu.make_async_copy(f_hbm, state.at[0, :, :, pl.ds(PAD, ex), :], load_sem.at[8])
    loads = [
        pltpu.make_async_copy(source, target, load_sem.at[n])
        for n, (source, target) in enumerate(
            (
                (rho_hbm, rho_ref),
                (speed_hbm, speed_ref),
                (kelvin_hbm, kelvin_ref),
                (obstacle_hbm, obstacle_ref),
                (surface_hbm, surface_ref),
                (porosity_hbm, porosity_ref),
                (patch_hbm, patch_ref),
                (holder_hbm, holder_ref),
            )
        )
    ]
    load.start()
    for copy in loads:
        copy.start()

    barrier = pltpu.get_barrier_semaphore()

    def inside(di, dj):
        a, b = i + di, j + dj
        return (a >= 0) & (a < nx) & (b >= 0) & (b < ny)

    xrecv[...] = jnp.zeros(xrecv.shape, jnp.float32)
    yrecv[...] = jnp.zeros(yrecv.shape, jnp.float32)
    crecv[...] = jnp.zeros(crecv.shape, jnp.float32)
    acc[...] = jnp.zeros(acc.shape, jnp.float32)

    mirrors = ((nx - 1 - i, j), (i, ny - 1 - j), (nx - 1 - i, ny - 1 - j))
    for dx, dy in DIRS:
        @pl.when(inside(dx, dy))
        def _():
            pl.semaphore_signal(barrier, inc=1, device_id=(i + dx, j + dy), device_id_type=MESH)
    far = max(nx, ny) - 1 > STEPS + 1
    if far:
        for d in range(1, nx):
            target = (lax.rem(i + d, nx), j)
            pl.semaphore_signal(barrier, inc=1, device_id=target, device_id_type=MESH)
        for target in mirrors:
            pl.semaphore_signal(barrier, inc=1, device_id=target, device_id_type=MESH)

    lane = lax.broadcasted_iota(jnp.int32, (8, ey), 1)

    for copy in loads:
        copy.wait()
    for z in range(height):
        fluid = 1.0 - obstacle_ref[z].astype(jnp.float32)
        for axis in range(3):
            const[axis, z] = speed_ref[axis, z] * fluid
        const[3, z] = 4.0 * CONDUCT_RATE * kelvin_ref[z] / rho_ref[z]
        const[4, z] = SOURCE_RATE * surface_ref[z].astype(jnp.float32)
        const[5, z] = fluid

    wide = 1 + (i > 0).astype(jnp.int32) + (i < nx - 1).astype(jnp.int32)
    deep = 1 + (j > 0).astype(jnp.int32) + (j < ny - 1).astype(jnp.int32)
    pl.semaphore_wait(barrier, wide * deep - 1 + (nx - 1 + len(mirrors) if far else 0))
    load.wait()

    def rim_copy(par, k):
        dx, dy = DIRS[k]
        if k < 2:
            src, dst = xsend.at[par, k], xrecv.at[par, k]
        elif k < 4:
            src, dst = ysend.at[par, k - 2], yrecv.at[par, k - 2]
        else:
            src, dst = csend.at[par, k - 4], crecv.at[par, k - 4]
        return pltpu.make_async_remote_copy(
            src_ref=src,
            dst_ref=dst,
            send_sem=send_sem.at[par, k],
            recv_sem=recv_sem.at[par, k],
            device_id=(i + dx, j + dy),
            device_id_type=MESH,
        )

    def send_rim(par):
        for side in range(2):
            for rt in range(tiles_of):
                packed = jnp.zeros((8, ey), jnp.float32)
                for p, pop in enumerate(YPOPS[side]):
                    for z in range(height):
                        q = p * height + z
                        value = state[par, pop, z, PAD + rt * 8 : PAD + rt * 8 + 8, :]
                        shift = q if side == 0 else (q + 1) % ey
                        if shift:
                            value = pltpu.roll(value, shift, 1)
                        packed = jnp.where(lane == q, value, packed)
                ysend[par, side, rt * 8 : rt * 8 + 8, :] = packed
                for k in range(4, 8):
                    dx, dy = DIRS[k]
                    if (0 if dy < 0 else 1) == side:
                        if dx < 0 and rt == 0:
                            csend[par, k - 4] = packed[0:1, :]
                        if dx > 0 and rt == tiles_of - 1:
                            csend[par, k - 4] = packed[7:8, :]
        for k in range(4, 8):
            @pl.when(inside(*DIRS[k]))
            def _():
                rim_copy(par, k).start()
        for k in range(2, 4):
            @pl.when(inside(*DIRS[k]))
            def _():
                rim_copy(par, k).start()
        for side in range(2):
            row = PAD if side == 0 else PAD + ex - 1
            for p, pop in enumerate(XPOPS[side]):
                for z in range(height):
                    q = p * height + z
                    xsend[par, side, q : q + 1, :] = state[par, pop, z, row : row + 1, :]
        for k in range(2):
            @pl.when(inside(*DIRS[k]))
            def _():
                rim_copy(par, k).start()

    def take_rim(par):
        for k in range(8):
            dx, dy = DIRS[k]

            @pl.when(inside(dx, dy))
            def _():
                rim_copy(par, k).wait_send()

            @pl.when(inside(-dx, -dy))
            def _():
                rim_copy(par, k).wait_recv()
        for side in range(2):
            row = PAD + ex if side == 0 else PAD - 1
            for p, pop in enumerate(XPOPS[side]):
                for z in range(height):
                    q = p * height + z
                    state[par, pop, z, row : row + 1, :] = xrecv[par, side, q : q + 1, :]
            yhalo[side, PAD : PAD + ex, :] = yrecv[par, side]
        for k in range(4, 8):
            dx, dy = DIRS[k]
            row = PAD + ex if dx < 0 else PAD - 1
            yhalo[0 if dy < 0 else 1, row : row + 1, :] = crecv[par, k - 4]

    def collide(par, z, rt):
        start = PAD + rt * 8

        def pull(pop):
            cx, cy, cz = velocity(pop)
            zz = z + cz
            if zz < 0 or zz >= height:
                return state[par, opposite(pop), z, start : start + 8, :]
            value = state[par, pop, zz, start + cx : start + cx + 8, :]
            if cy:
                side = 0 if cy == 1 else 1
                q = YPOPS[side].index(pop) * height + zz
                edge = yhalo[side, start + cx : start + cx + 8, :]
                last = ey - 1 if cy == 1 else 0
                shift = (last - q) % ey
                if shift:
                    edge = pltpu.roll(edge, shift, 1)
                value = pltpu.roll(value, (-cy) % ey, 1)
                value = jnp.where(lane == last, edge, value)
            return value

        rows = slice(rt * 8, rt * 8 + 8)
        ux, uy, uz = const[0, z, rows, :], const[1, z, rows, :], const[2, z, rows, :]
        coupling = const[3, z, rows, :]
        source = const[4, z, rows, :]
        fluid = const[5, z, rows, :] > 0.5

        b = [pull(FLOW + k) for k in range(7)]
        tsum = V0 * b[0] + V1 * ((b[1] + b[2]) + (b[3] + b[4]) + (b[5] + b[6]))
        qx, qy, qz = V1 * (b[1] - b[2]), V1 * (b[3] - b[4]), V1 * (b[5] - b[6])
        qu = qx * ux + qy * uy + qz * uz
        warm = CONDUCT_RATE * (tsum + 4.0 * qu) + source
        for k in range(7):
            state[1 - par, FLOW + k, z, start : start + 8, :] = (1.0 - CONDUCT_RATE) * b[k] + warm

        a = [pull(k) for k in range(FLOW)]
        sm = {k: a[k] + a[k + 1] for k in range(1, FLOW, 2)}
        df = {k: a[k] - a[k + 1] for k in range(1, FLOW, 2)}
        sx = (3.0 * W1) * df[1] + (3.0 * W2) * ((df[7] + df[9]) + (df[11] + df[13]))
        sy = (3.0 * W1) * df[3] + (3.0 * W2) * ((df[7] - df[9]) + (df[15] + df[17]))
        sz = (3.0 * W1) * df[5] + (3.0 * W2) * ((df[11] - df[13]) + (df[15] - df[17]))
        xy, xz, yz = sm[7] + sm[9], sm[11] + sm[13], sm[15] + sm[17]
        mass = W0 * a[0] + W1 * (sm[1] + sm[3] + sm[5]) + W2 * (xy + xz + yz)
        quad = (
            (ux * ux) * (W1 * sm[1] + W2 * (xy + xz))
            + (uy * uy) * (W1 * sm[3] + W2 * (xy + yz))
            + (uz * uz) * (W1 * sm[5] + W2 * (xz + yz))
            + (2.0 * W2)
            * (
                (ux * uy) * (sm[7] - sm[9])
                + (ux * uz) * (sm[11] - sm[13])
                + (uy * uz) * (sm[15] - sm[17])
            )
        )
        square = ux * ux + uy * uy + uz * uz
        scalar = mass * (1.0 - 1.5 * square) + 4.5 * quad
        base = OMEGA_FLOW * scalar - coupling * qu
        gx = OMEGA_FLOW * sx + coupling * qx
        gy = OMEGA_FLOW * sy + coupling * qy
        gz = OMEGA_FLOW * sz + coupling * qz
        along = {
            1: gx,
            3: gy,
            5: gz,
            7: gx + gy,
            9: gx - gy,
            11: gx + gz,
            13: gx - gz,
            15: gy + gz,
            17: gy - gz,
        }
        keep = 1.0 - OMEGA_FLOW

        def put(pop, value):
            state[1 - par, pop, z, start : start + 8, :] = value

        put(0, jnp.where(fluid, keep * a[0] + base, a[0]))
        for k in range(1, FLOW, 2):
            put(k, jnp.where(fluid, keep * a[k] + (base + along[k]), a[k + 1]))
            put(k + 1, jnp.where(fluid, keep * a[k + 1] + (base - along[k]), a[k]))
        return HEAT_RATE * tsum - rho_ref[z, rows, :] * (ux * sx + uy * sy + uz * sz)

    send_rim(0)

    number = lax.broadcasted_iota(jnp.int32, (blocks, ey), 0)
    below = (
        lax.broadcasted_iota(jnp.int32, (ey, ey), 0) < lax.broadcasted_iota(jnp.int32, (ey, ey), 1)
    ).astype(jnp.bfloat16)
    place = lax.broadcasted_iota(jnp.int32, (TILE, ey), 0).astype(jnp.float32)
    running = jnp.zeros((blocks, 1), jnp.float32)
    for x in range(ex):
        hits = (patch_ref[x : x + 1, :] == number).astype(jnp.float32)
        earlier = jnp.dot(
            hits.astype(jnp.bfloat16), below, preferred_element_type=jnp.float32
        )
        rank = jnp.sum(hits * (earlier + running), axis=0, keepdims=True)
        running = running + jnp.sum(hits, axis=1, keepdims=True)
        hot[:, x * ey : (x + 1) * ey] = (place == rank).astype(jnp.bfloat16)
        label_rows[:, x * ey : (x + 1) * ey] = hits

    def gathered(field):
        columns = jnp.concatenate(
            [
                label_rows[:, x * ey : (x + 1) * ey] * field[x : x + 1, :]
                for x in range(ex)
            ],
            axis=1,
        )
        parts = jnp.concatenate(split3(columns), axis=0)
        result = lax.dot_general(
            parts, hot[...], (((1,), (1,)), ((), ())), preferred_element_type=jnp.float32
        )
        return result[:blocks] + result[blocks : 2 * blocks] + result[2 * blocks :]

    design = gathered(porosity_ref[...])

    owner_row = jnp.concatenate(
        [
            holder_ref[...].astype(jnp.float32),
            jnp.zeros((1, TILE - blocks), jnp.float32),
        ],
        axis=1,
    )
    rows_of = lax.broadcasted_iota(jnp.int32, (blocks, TILE), 0)
    lanes_of = lax.broadcasted_iota(jnp.int32, (blocks, TILE), 1)
    diagonal = (rows_of == lanes_of).astype(jnp.float32)
    owner = jnp.sum(owner_row * diagonal, axis=1, keepdims=True)
    same = ((owner == owner_row) & (rows_of < lanes_of) & (lanes_of < blocks)).astype(jnp.float32)
    rank_row = jnp.sum(same, axis=0, keepdims=True)
    slot_row = owner_row * float(cap) + rank_row
    slots = nx * cap
    choose = (
        (lax.broadcasted_iota(jnp.int32, (slots, TILE), 0).astype(jnp.float32) == slot_row)
        & (lax.broadcasted_iota(jnp.int32, (slots, TILE), 1) < blocks)
    ).astype(jnp.bfloat16)

    def step(s, carry):
        par = lax.rem(s, 2)
        take_rim(par)
        for rt in range(tiles_of):
            sens = collide(par, 0, rt)
            for z in range(1, height):
                sens = sens + collide(par, z, rt)
            acc[rt * 8 : rt * 8 + 8, :] += sens

        @pl.when(s < STEPS - 1)
        def _():
            send_rim(1 - par)

        return carry

    lax.fori_loop(0, STEPS, step, 0)

    last = STEPS % 2
    store = pltpu.make_async_copy(state.at[last, :, :, pl.ds(PAD, ex), :], out_hbm, store_sem)
    store.start()

    column[...] = acc[...]

    def mirror_copy(m):
        return pltpu.make_async_remote_copy(
            src_ref=column,
            dst_ref=mirror.at[m],
            send_sem=msend_sem.at[m],
            recv_sem=mrecv_sem.at[m],
            device_id=mirrors[m],
            device_id_type=MESH,
        )

    for m in (2, 1, 0):
        mirror_copy(m).start()
    for m in range(3):
        mirror_copy(m).wait()
    for x in range(ex):
        flip_a[x : x + 1, :] = mirror[0, ex - 1 - x : ex - x, :]
        flip_b[x : x + 1, :] = mirror[2, ex - 1 - x : ex - x, :]
    reverse = (
        lax.broadcasted_iota(jnp.int32, (ey, ey), 0) + lax.broadcasted_iota(jnp.int32, (ey, ey), 1)
        == ey - 1
    ).astype(jnp.bfloat16)
    turned = jnp.dot(
        jnp.concatenate(split3(mirror[1] + flip_b[...]), axis=0),
        reverse,
        preferred_element_type=jnp.float32,
    )
    symmetric = (
        column[...] + flip_a[...] + (turned[:ex] + turned[ex : 2 * ex] + turned[2 * ex :])
    )
    sens = gathered(symmetric)
    spread = jnp.sqrt(jnp.mean(sens * sens, axis=1, keepdims=True) + 1e-06)
    fresh = jnp.clip(design - STEP_SIZE * sens / spread, 0.0, 1.0)
    padded = jnp.concatenate([fresh, jnp.zeros((TILE - blocks, TILE), jnp.float32)], axis=0)
    parts = jnp.concatenate(split3(padded), axis=1)
    sent = jnp.dot(choose, parts, preferred_element_type=jnp.float32)
    sent = sent[:, :TILE] + sent[:, TILE : 2 * TILE] + sent[:, 2 * TILE :]
    for o in range(nx):
        outgoing[o] = sent[o * cap : (o + 1) * cap, :]

    def owner_copy(d):
        target = lax.rem(i + d, nx)
        return pltpu.make_async_remote_copy(
            src_ref=outgoing.at[target],
            dst_ref=received.at[i],
            send_sem=asend_sem.at[d],
            recv_sem=arecv_sem.at[d],
            device_id=(target, j),
            device_id_type=MESH,
        )

    def arriving(d):
        origin = lax.rem(i + nx - d, nx)
        return pltpu.make_async_remote_copy(
            src_ref=outgoing.at[origin],
            dst_ref=received.at[origin],
            send_sem=asend_sem.at[d],
            recv_sem=arecv_sem.at[d],
            device_id=(origin, j),
            device_id_type=MESH,
        )

    for d in range(1, nx):
        owner_copy(d).start()
    received[i] = outgoing[i]
    for d in range(1, nx):
        owner_copy(d).wait_send()
        arriving(d).wait_recv()
    for o in range(nx):
        tiles_ref[o * cap : (o + 1) * cap, :] = received[o]
    store.wait()


def on_device(
    dual_distributions,
    primal_fluid_rho,
    forward_flow_speed,
    primal_kelvin_values,
    obstacle_mask,
    objective_surface_mask,
    pillar_porosity,
    pillar_design_patch,
    patch_holder,
):
    nx, ny = lax.axis_size("gx"), lax.axis_size("gy")
    pops, height, ex, ey = dual_distributions.shape
    blocks = ex * ey // TILE
    cap = max(2, 2 * blocks // nx)
    nxp, nyp = len(XPOPS[0]), len(YPOPS[0])
    f32 = jnp.float32
    vmem = pl.BlockSpec(memory_space=pltpu.VMEM)
    hbm = pl.BlockSpec(memory_space=pl.ANY)
    return pl.pallas_call(
        functools.partial(body, (nx, ny, height, ex, ey, blocks, cap)),
        out_shape=(
            jax.ShapeDtypeStruct(dual_distributions.shape, f32),
            jax.ShapeDtypeStruct((nx * cap, TILE), f32),
        ),
        in_specs=[hbm] * 9,
        out_specs=(hbm, vmem),
        scratch_shapes=[
            pltpu.VMEM(primal_fluid_rho.shape, f32),
            pltpu.VMEM(forward_flow_speed.shape, f32),
            pltpu.VMEM(primal_kelvin_values.shape, f32),
            pltpu.VMEM(obstacle_mask.shape, jnp.int32),
            pltpu.VMEM(objective_surface_mask.shape, jnp.int32),
            pltpu.VMEM(pillar_porosity.shape, f32),
            pltpu.VMEM(pillar_design_patch.shape, jnp.int32),
            pltpu.VMEM((1, blocks), jnp.int32),
            pltpu.VMEM((2, pops, height, ex + 2 * PAD, ey), f32),
            pltpu.VMEM((6, height, ex, ey), f32),
            pltpu.VMEM((ex, ey), f32),
            pltpu.VMEM((2, 2, nxp * height, ey), f32),
            pltpu.VMEM((2, 2, nxp * height, ey), f32),
            pltpu.VMEM((2, 2, ex, ey), f32),
            pltpu.VMEM((2, 2, ex, ey), f32),
            pltpu.VMEM((2, 4, 1, ey), f32),
            pltpu.VMEM((2, 4, 1, ey), f32),
            pltpu.VMEM((2, ex + 2 * PAD, ey), f32),
            pltpu.VMEM((TILE, ex * ey), jnp.bfloat16),
            pltpu.VMEM((blocks, ex * ey), f32),
            pltpu.VMEM((ex, ey), f32),
            pltpu.VMEM((ex, ey), f32),
            pltpu.VMEM((ex, ey), f32),
            pltpu.VMEM((3, ex, ey), f32),
            pltpu.VMEM((nx, cap, TILE), f32),
            pltpu.VMEM((nx, cap, TILE), f32),
            pltpu.SemaphoreType.DMA((9,)),
            pltpu.SemaphoreType.DMA,
            pltpu.SemaphoreType.DMA((2, 8)),
            pltpu.SemaphoreType.DMA((2, 8)),
            pltpu.SemaphoreType.DMA((3,)),
            pltpu.SemaphoreType.DMA((3,)),
            pltpu.SemaphoreType.DMA((nx,)),
            pltpu.SemaphoreType.DMA((nx,)),
        ],
        compiler_params=pltpu.CompilerParams(collective_id=0, has_side_effects=True),
    )(
        dual_distributions,
        primal_fluid_rho,
        forward_flow_speed,
        primal_kelvin_values,
        obstacle_mask,
        objective_surface_mask,
        pillar_porosity,
        pillar_design_patch,
        patch_holder.T,
    )


def solution(mesh):
    in_specs = (
        P(None, None, "gx", "gy"),
        P(None, "gx", "gy"),
        P(None, None, "gx", "gy"),
        P(None, "gx", "gy"),
        P(None, "gx", "gy"),
        P(None, "gx", "gy"),
        P("gx", "gy"),
        P("gx", "gy"),
        P(("gx", "gy"), None),
    )
    out_specs = (P(None, None, "gx", "gy"), P(("gx", "gy"), None))
    return jax.shard_map(
        on_device, mesh=mesh, in_specs=in_specs, out_specs=out_specs, check_vma=False
    )
```

```python
import functools

import jax
import jax.numpy as jnp
from jax import lax
from jax.experimental import pallas as pl
from jax.experimental.pallas import tpu as pltpu
from jax.sharding import PartitionSpec as P

STEPS = 6
TILE = 128

VELOCITIES = (
    (0, 0, 0),
    (1, 0, 0),
    (-1, 0, 0),
    (0, 1, 0),
    (0, -1, 0),
    (0, 0, 1),
    (0, 0, -1),
    (1, 1, 0),
    (-1, -1, 0),
    (1, -1, 0),
    (-1, 1, 0),
    (1, 0, 1),
    (-1, 0, -1),
    (1, 0, -1),
    (-1, 0, 1),
    (0, 1, 1),
    (0, -1, -1),
    (0, 1, -1),
    (0, -1, 1),
)
W0, W1, W2 = 1.0 / 3.0, 1.0 / 18.0, 1.0 / 36.0
V0, V1 = 0.25, 0.125
FLOW = 19
POPS = 26
OMEGA_FLOW = 1.6
CONDUCT_RATE = 1.2
SOURCE_RATE = 0.5
HEAT_RATE = 0.1
STEP_SIZE = 0.1

DIRS = ((-1, 0), (1, 0), (0, -1), (0, 1), (-1, -1), (1, -1), (-1, 1), (1, 1))
MESH = pl.DeviceIdType.MESH
PAD = 8


def velocity(pop):
    return VELOCITIES[pop if pop < FLOW else pop - FLOW]


def opposite(pop):
    base = 0 if pop < FLOW else FLOW
    within = pop - base
    if within == 0:
        return pop
    return base + (within + 1 if within % 2 == 1 else within - 1)


def moving(axis, sign):
    return [pop for pop in range(POPS) if velocity(pop)[axis] == sign]


XPOPS = (moving(0, 1), moving(0, -1))
YPOPS = (moving(1, 1), moving(1, -1))


def split3(value):
    high = value.astype(jnp.bfloat16)
    rest = value - high.astype(jnp.float32)
    middle = rest.astype(jnp.bfloat16)
    low = (rest - middle.astype(jnp.float32)).astype(jnp.bfloat16)
    return high, middle, low


def body(
    sizes,
    f_hbm,
    rho_hbm,
    speed_hbm,
    kelvin_hbm,
    obstacle_hbm,
    surface_hbm,
    porosity_hbm,
    patch_hbm,
    holder_hbm,
    out_ref,
    tiles_ref,
    rho_ref,
    speed_ref,
    kelvin_ref,
    obstacle_ref,
    surface_ref,
    porosity_ref,
    patch_ref,
    holder_ref,
    state,
    const,
    acc,
    xsend,
    xrecv,
    ysend,
    yrecv,
    csend,
    crecv,
    yhalo,
    hot,
    label_rows,
    flip_a,
    flip_b,
    column,
    mirror,
    outgoing,
    received,
    load_sem,
    send_sem,
    recv_sem,
    msend_sem,
    mrecv_sem,
    asend_sem,
    arecv_sem,
):
    nx, ny, height, ex, ey, blocks, cap = sizes
    i = lax.axis_index("gx")
    j = lax.axis_index("gy")
    tiles_of = ex // 8

    load = pltpu.make_async_copy(f_hbm, state.at[0, :, :, pl.ds(PAD, ex), :], load_sem.at[8])
    loads = [
        pltpu.make_async_copy(source, target, load_sem.at[n])
        for n, (source, target) in enumerate(
            (
                (rho_hbm, rho_ref),
                (speed_hbm, speed_ref),
                (kelvin_hbm, kelvin_ref),
                (obstacle_hbm, obstacle_ref),
                (surface_hbm, surface_ref),
                (porosity_hbm, porosity_ref),
                (patch_hbm, patch_ref),
                (holder_hbm, holder_ref),
            )
        )
    ]
    load.start()
    for copy in loads:
        copy.start()

    barrier = pltpu.get_barrier_semaphore()

    def inside(di, dj):
        a, b = i + di, j + dj
        return (a >= 0) & (a < nx) & (b >= 0) & (b < ny)

    xrecv[...] = jnp.zeros(xrecv.shape, jnp.float32)
    yrecv[...] = jnp.zeros(yrecv.shape, jnp.float32)
    crecv[...] = jnp.zeros(crecv.shape, jnp.float32)
    acc[...] = jnp.zeros(acc.shape, jnp.float32)

    mirrors = ((nx - 1 - i, j), (i, ny - 1 - j), (nx - 1 - i, ny - 1 - j))
    for dx, dy in DIRS:
        @pl.when(inside(dx, dy))
        def _():
            pl.semaphore_signal(barrier, inc=1, device_id=(i + dx, j + dy), device_id_type=MESH)
    far = max(nx, ny) - 1 > STEPS + 1
    if far:
        for d in range(1, nx):
            target = (lax.rem(i + d, nx), j)
            pl.semaphore_signal(barrier, inc=1, device_id=target, device_id_type=MESH)
        for target in mirrors:
            pl.semaphore_signal(barrier, inc=1, device_id=target, device_id_type=MESH)

    lane = lax.broadcasted_iota(jnp.int32, (8, ey), 1)

    for copy in loads:
        copy.wait()
    for z in range(height):
        fluid = 1.0 - obstacle_ref[z].astype(jnp.float32)
        for axis in range(3):
            const[axis, z] = speed_ref[axis, z] * fluid
        const[3, z] = 4.0 * CONDUCT_RATE * kelvin_ref[z] / rho_ref[z]
        const[4, z] = SOURCE_RATE * surface_ref[z].astype(jnp.float32)
        const[5, z] = fluid

    wide = 1 + (i > 0).astype(jnp.int32) + (i < nx - 1).astype(jnp.int32)
    deep = 1 + (j > 0).astype(jnp.int32) + (j < ny - 1).astype(jnp.int32)
    pl.semaphore_wait(barrier, wide * deep - 1 + (nx - 1 + len(mirrors) if far else 0))
    load.wait()

    def rim_copy(par, k):
        dx, dy = DIRS[k]
        if k < 2:
            src, dst = xsend.at[par, k], xrecv.at[par, k]
        elif k < 4:
            src, dst = ysend.at[par, k - 2], yrecv.at[par, k - 2]
        else:
            src, dst = csend.at[par, k - 4], crecv.at[par, k - 4]
        return pltpu.make_async_remote_copy(
            src_ref=src,
            dst_ref=dst,
            send_sem=send_sem.at[par, k],
            recv_sem=recv_sem.at[par, k],
            device_id=(i + dx, j + dy),
            device_id_type=MESH,
        )

    def send_rim(par):
        for side in range(2):
            for rt in range(tiles_of):
                packed = jnp.zeros((8, ey), jnp.float32)
                for p, pop in enumerate(YPOPS[side]):
                    for z in range(height):
                        q = p * height + z
                        value = state[par, pop, z, PAD + rt * 8 : PAD + rt * 8 + 8, :]
                        shift = q if side == 0 else (q + 1) % ey
                        if shift:
                            value = pltpu.roll(value, shift, 1)
                        packed = jnp.where(lane == q, value, packed)
                ysend[par, side, rt * 8 : rt * 8 + 8, :] = packed
                for k in range(4, 8):
                    dx, dy = DIRS[k]
                    if (0 if dy < 0 else 1) == side:
                        if dx < 0 and rt == 0:
                            csend[par, k - 4] = packed[0:1, :]
                        if dx > 0 and rt == tiles_of - 1:
                            csend[par, k - 4] = packed[7:8, :]
        for k in range(4, 8):
            @pl.when(inside(*DIRS[k]))
            def _():
                rim_copy(par, k).start()
        for k in range(2, 4):
            @pl.when(inside(*DIRS[k]))
            def _():
                rim_copy(par, k).start()
        for side in range(2):
            row = PAD if side == 0 else PAD + ex - 1
            for p, pop in enumerate(XPOPS[side]):
                for z in range(height):
                    q = p * height + z
                    xsend[par, side, q : q + 1, :] = state[par, pop, z, row : row + 1, :]
        for k in range(2):
            @pl.when(inside(*DIRS[k]))
            def _():
                rim_copy(par, k).start()

    def take_rim(par):
        for k in range(8):
            dx, dy = DIRS[k]

            @pl.when(inside(dx, dy))
            def _():
                rim_copy(par, k).wait_send()

            @pl.when(inside(-dx, -dy))
            def _():
                rim_copy(par, k).wait_recv()
        for side in range(2):
            row = PAD + ex if side == 0 else PAD - 1
            for p, pop in enumerate(XPOPS[side]):
                for z in range(height):
                    q = p * height + z
                    state[par, pop, z, row : row + 1, :] = xrecv[par, side, q : q + 1, :]
            yhalo[side, PAD : PAD + ex, :] = yrecv[par, side]
        for k in range(4, 8):
            dx, dy = DIRS[k]
            row = PAD + ex if dx < 0 else PAD - 1
            yhalo[0 if dy < 0 else 1, row : row + 1, :] = crecv[par, k - 4]

    def collide(par, z, rt, put, moments_only=False):
        start = PAD + rt * 8

        def pull(pop):
            cx, cy, cz = velocity(pop)
            zz = z + cz
            if zz < 0 or zz >= height:
                return state[par, opposite(pop), z, start : start + 8, :]
            value = state[par, pop, zz, start + cx : start + cx + 8, :]
            if cy:
                side = 0 if cy == 1 else 1
                q = YPOPS[side].index(pop) * height + zz
                edge = yhalo[side, start + cx : start + cx + 8, :]
                last = ey - 1 if cy == 1 else 0
                shift = (last - q) % ey
                if shift:
                    edge = pltpu.roll(edge, shift, 1)
                value = pltpu.roll(value, (-cy) % ey, 1)
                value = jnp.where(lane == last, edge, value)
            return value

        rows = slice(rt * 8, rt * 8 + 8)
        ux, uy, uz = const[0, z, rows, :], const[1, z, rows, :], const[2, z, rows, :]
        coupling = const[3, z, rows, :]
        source = const[4, z, rows, :]
        fluid = const[5, z, rows, :] > 0.5

        b = [pull(FLOW + k) for k in range(7)]
        tsum = V0 * b[0] + V1 * ((b[1] + b[2]) + (b[3] + b[4]) + (b[5] + b[6]))
        qx, qy, qz = V1 * (b[1] - b[2]), V1 * (b[3] - b[4]), V1 * (b[5] - b[6])
        qu = qx * ux + qy * uy + qz * uz
        warm = CONDUCT_RATE * (tsum + 4.0 * qu) + source
        if not moments_only:
            for k in range(7):
                put(FLOW + k, z, rt, (1.0 - CONDUCT_RATE) * b[k] + warm)

        a = [None if moments_only and k == 0 else pull(k) for k in range(FLOW)]
        sm = {k: a[k] + a[k + 1] for k in range(1, FLOW, 2)}
        df = {k: a[k] - a[k + 1] for k in range(1, FLOW, 2)}
        sx = (3.0 * W1) * df[1] + (3.0 * W2) * ((df[7] + df[9]) + (df[11] + df[13]))
        sy = (3.0 * W1) * df[3] + (3.0 * W2) * ((df[7] - df[9]) + (df[15] + df[17]))
        sz = (3.0 * W1) * df[5] + (3.0 * W2) * ((df[11] - df[13]) + (df[15] - df[17]))
        sens = HEAT_RATE * tsum - rho_ref[z, rows, :] * (ux * sx + uy * sy + uz * sz)
        if moments_only:
            return sens
        xy, xz, yz = sm[7] + sm[9], sm[11] + sm[13], sm[15] + sm[17]
        mass = W0 * a[0] + W1 * (sm[1] + sm[3] + sm[5]) + W2 * (xy + xz + yz)
        quad = (
            (ux * ux) * (W1 * sm[1] + W2 * (xy + xz))
            + (uy * uy) * (W1 * sm[3] + W2 * (xy + yz))
            + (uz * uz) * (W1 * sm[5] + W2 * (xz + yz))
            + (2.0 * W2)
            * (
                (ux * uy) * (sm[7] - sm[9])
                + (ux * uz) * (sm[11] - sm[13])
                + (uy * uz) * (sm[15] - sm[17])
            )
        )
        square = ux * ux + uy * uy + uz * uz
        scalar = mass * (1.0 - 1.5 * square) + 4.5 * quad
        base = OMEGA_FLOW * scalar - coupling * qu
        gx = OMEGA_FLOW * sx + coupling * qx
        gy = OMEGA_FLOW * sy + coupling * qy
        gz = OMEGA_FLOW * sz + coupling * qz
        along = {
            1: gx,
            3: gy,
            5: gz,
            7: gx + gy,
            9: gx - gy,
            11: gx + gz,
            13: gx - gz,
            15: gy + gz,
            17: gy - gz,
        }
        keep = 1.0 - OMEGA_FLOW

        put(0, z, rt, jnp.where(fluid, keep * a[0] + base, a[0]))
        for k in range(1, FLOW, 2):
            put(k, z, rt, jnp.where(fluid, keep * a[k] + (base + along[k]), a[k + 1]))
            put(k + 1, z, rt, jnp.where(fluid, keep * a[k + 1] + (base - along[k]), a[k]))
        return sens

    send_rim(0)

    number = lax.broadcasted_iota(jnp.int32, (blocks, ey), 0)
    below = (
        lax.broadcasted_iota(jnp.int32, (ey, ey), 0) < lax.broadcasted_iota(jnp.int32, (ey, ey), 1)
    ).astype(jnp.bfloat16)
    place = lax.broadcasted_iota(jnp.int32, (TILE, ey), 0).astype(jnp.float32)
    running = jnp.zeros((blocks, 1), jnp.float32)
    for x in range(ex):
        hits = (patch_ref[x : x + 1, :] == number).astype(jnp.float32)
        earlier = jnp.dot(
            hits.astype(jnp.bfloat16), below, preferred_element_type=jnp.float32
        )
        rank = jnp.sum(hits * (earlier + running), axis=0, keepdims=True)
        running = running + jnp.sum(hits, axis=1, keepdims=True)
        hot[:, x * ey : (x + 1) * ey] = (place == rank).astype(jnp.bfloat16)
        label_rows[:, x * ey : (x + 1) * ey] = hits

    def gathered(field):
        columns = jnp.concatenate(
            [
                label_rows[:, x * ey : (x + 1) * ey] * field[x : x + 1, :]
                for x in range(ex)
            ],
            axis=1,
        )
        parts = jnp.concatenate(split3(columns), axis=0)
        result = lax.dot_general(
            parts, hot[...], (((1,), (1,)), ((), ())), preferred_element_type=jnp.float32
        )
        return result[:blocks] + result[blocks : 2 * blocks] + result[2 * blocks :]

    design = gathered(porosity_ref[...])

    owner_row = jnp.concatenate(
        [
            holder_ref[...].astype(jnp.float32),
            jnp.zeros((1, TILE - blocks), jnp.float32),
        ],
        axis=1,
    )
    rows_of = lax.broadcasted_iota(jnp.int32, (blocks, TILE), 0)
    lanes_of = lax.broadcasted_iota(jnp.int32, (blocks, TILE), 1)
    diagonal = (rows_of == lanes_of).astype(jnp.float32)
    owner = jnp.sum(owner_row * diagonal, axis=1, keepdims=True)
    same = ((owner == owner_row) & (rows_of < lanes_of) & (lanes_of < blocks)).astype(jnp.float32)
    rank_row = jnp.sum(same, axis=0, keepdims=True)
    slot_row = owner_row * float(cap) + rank_row
    slots = nx * cap
    choose = (
        (lax.broadcasted_iota(jnp.int32, (slots, TILE), 0).astype(jnp.float32) == slot_row)
        & (lax.broadcasted_iota(jnp.int32, (slots, TILE), 1) < blocks)
    ).astype(jnp.bfloat16)

    def step(s, carry):
        par = lax.rem(s, 2)

        def put(pop, z, rt, value):
            start = PAD + rt * 8
            state[1 - par, pop, z, start : start + 8, :] = value

        take_rim(par)
        for rt in range(tiles_of):
            sens = collide(par, 0, rt, put)
            for z in range(1, height):
                sens = sens + collide(par, z, rt, put)
            acc[rt * 8 : rt * 8 + 8, :] += sens
        send_rim(1 - par)
        return carry

    lax.fori_loop(0, STEPS - 1, step, 0)

    last = (STEPS - 1) % 2

    def put_out(pop, z, rt, value):
        out_ref[pop, z, rt * 8 : rt * 8 + 8, :] = value

    take_rim(last)
    for rt in range(tiles_of):
        sens = collide(last, 0, rt, None, True)
        for z in range(1, height):
            sens = sens + collide(last, z, rt, None, True)
        column[rt * 8 : rt * 8 + 8, :] = acc[rt * 8 : rt * 8 + 8, :] + sens

    def mirror_copy(m):
        return pltpu.make_async_remote_copy(
            src_ref=column,
            dst_ref=mirror.at[m],
            send_sem=msend_sem.at[m],
            recv_sem=mrecv_sem.at[m],
            device_id=mirrors[m],
            device_id_type=MESH,
        )

    for m in (2, 1, 0):
        mirror_copy(m).start()
    for rt in range(tiles_of):
        for z in range(height):
            collide(last, z, rt, put_out)
    for m in range(3):
        mirror_copy(m).wait()
    for x in range(ex):
        flip_a[x : x + 1, :] = mirror[0, ex - 1 - x : ex - x, :]
        flip_b[x : x + 1, :] = mirror[2, ex - 1 - x : ex - x, :]
    reverse = (
        lax.broadcasted_iota(jnp.int32, (ey, ey), 0) + lax.broadcasted_iota(jnp.int32, (ey, ey), 1)
        == ey - 1
    ).astype(jnp.bfloat16)
    turned = jnp.dot(
        jnp.concatenate(split3(mirror[1] + flip_b[...]), axis=0),
        reverse,
        preferred_element_type=jnp.float32,
    )
    symmetric = (
        column[...] + flip_a[...] + (turned[:ex] + turned[ex : 2 * ex] + turned[2 * ex :])
    )
    sens = gathered(symmetric)
    spread = jnp.sqrt(jnp.mean(sens * sens, axis=1, keepdims=True) + 1e-06)
    fresh = jnp.clip(design - STEP_SIZE * sens / spread, 0.0, 1.0)
    padded = jnp.concatenate([fresh, jnp.zeros((TILE - blocks, TILE), jnp.float32)], axis=0)
    parts = jnp.concatenate(split3(padded), axis=1)
    sent = jnp.dot(choose, parts, preferred_element_type=jnp.float32)
    sent = sent[:, :TILE] + sent[:, TILE : 2 * TILE] + sent[:, 2 * TILE :]
    for o in range(nx):
        outgoing[o] = sent[o * cap : (o + 1) * cap, :]

    def owner_copy(d):
        target = lax.rem(i + d, nx)
        return pltpu.make_async_remote_copy(
            src_ref=outgoing.at[target],
            dst_ref=received.at[i],
            send_sem=asend_sem.at[d],
            recv_sem=arecv_sem.at[d],
            device_id=(target, j),
            device_id_type=MESH,
        )

    def arriving(d):
        origin = lax.rem(i + nx - d, nx)
        return pltpu.make_async_remote_copy(
            src_ref=outgoing.at[origin],
            dst_ref=received.at[origin],
            send_sem=asend_sem.at[d],
            recv_sem=arecv_sem.at[d],
            device_id=(origin, j),
            device_id_type=MESH,
        )

    for d in range(1, nx):
        owner_copy(d).start()
    received[i] = outgoing[i]
    for d in range(1, nx):
        owner_copy(d).wait_send()
        arriving(d).wait_recv()
    for o in range(nx):
        tiles_ref[o * cap : (o + 1) * cap, :] = received[o]


def on_device(
    dual_distributions,
    primal_fluid_rho,
    forward_flow_speed,
    primal_kelvin_values,
    obstacle_mask,
    objective_surface_mask,
    pillar_porosity,
    pillar_design_patch,
    patch_holder,
):
    nx, ny = lax.axis_size("gx"), lax.axis_size("gy")
    pops, height, ex, ey = dual_distributions.shape
    blocks = ex * ey // TILE
    cap = max(2, 2 * blocks // nx)
    nxp, nyp = len(XPOPS[0]), len(YPOPS[0])
    f32 = jnp.float32
    vmem = pl.BlockSpec(memory_space=pltpu.VMEM)
    hbm = pl.BlockSpec(memory_space=pl.ANY)
    return pl.pallas_call(
        functools.partial(body, (nx, ny, height, ex, ey, blocks, cap)),
        out_shape=(
            pltpu.VMEM(dual_distributions.shape, f32),
            pltpu.VMEM((nx * cap, TILE), f32),
        ),
        in_specs=[hbm] * 9,
        out_specs=(vmem, vmem),
        scratch_shapes=[
            pltpu.VMEM(primal_fluid_rho.shape, f32),
            pltpu.VMEM(forward_flow_speed.shape, f32),
            pltpu.VMEM(primal_kelvin_values.shape, f32),
            pltpu.VMEM(obstacle_mask.shape, jnp.int32),
            pltpu.VMEM(objective_surface_mask.shape, jnp.int32),
            pltpu.VMEM(pillar_porosity.shape, f32),
            pltpu.VMEM(pillar_design_patch.shape, jnp.int32),
            pltpu.VMEM((1, blocks), jnp.int32),
            pltpu.VMEM((2, pops, height, ex + 2 * PAD, ey), f32),
            pltpu.VMEM((6, height, ex, ey), f32),
            pltpu.VMEM((ex, ey), f32),
            pltpu.VMEM((2, 2, nxp * height, ey), f32),
            pltpu.VMEM((2, 2, nxp * height, ey), f32),
            pltpu.VMEM((2, 2, ex, ey), f32),
            pltpu.VMEM((2, 2, ex, ey), f32),
            pltpu.VMEM((2, 4, 1, ey), f32),
            pltpu.VMEM((2, 4, 1, ey), f32),
            pltpu.VMEM((2, ex + 2 * PAD, ey), f32),
            pltpu.VMEM((TILE, ex * ey), jnp.bfloat16),
            pltpu.VMEM((blocks, ex * ey), f32),
            pltpu.VMEM((ex, ey), f32),
            pltpu.VMEM((ex, ey), f32),
            pltpu.VMEM((ex, ey), f32),
            pltpu.VMEM((3, ex, ey), f32),
            pltpu.VMEM((nx, cap, TILE), f32),
            pltpu.VMEM((nx, cap, TILE), f32),
            pltpu.SemaphoreType.DMA((9,)),
            pltpu.SemaphoreType.DMA((2, 8)),
            pltpu.SemaphoreType.DMA((2, 8)),
            pltpu.SemaphoreType.DMA((3,)),
            pltpu.SemaphoreType.DMA((3,)),
            pltpu.SemaphoreType.DMA((nx,)),
            pltpu.SemaphoreType.DMA((nx,)),
        ],
        compiler_params=pltpu.CompilerParams(collective_id=0, has_side_effects=True),
    )(
        dual_distributions,
        primal_fluid_rho,
        forward_flow_speed,
        primal_kelvin_values,
        obstacle_mask,
        objective_surface_mask,
        pillar_porosity,
        pillar_design_patch,
        patch_holder.T,
    )


def solution(mesh):
    in_specs = (
        P(None, None, "gx", "gy"),
        P(None, "gx", "gy"),
        P(None, None, "gx", "gy"),
        P(None, "gx", "gy"),
        P(None, "gx", "gy"),
        P(None, "gx", "gy"),
        P("gx", "gy"),
        P("gx", "gy"),
        P(("gx", "gy"), None),
    )
    out_specs = (P(None, None, "gx", "gy"), P(("gx", "gy"), None))
    return jax.shard_map(
        on_device, mesh=mesh, in_specs=in_specs, out_specs=out_specs, check_vma=False
    )
```

```python
import functools

import jax
import jax.numpy as jnp
from jax import lax
from jax.experimental import pallas as pl
from jax.experimental.pallas import tpu as pltpu
from jax.sharding import PartitionSpec as P

STEPS = 6
TILE = 128

VELOCITIES = (
    (0, 0, 0),
    (1, 0, 0),
    (-1, 0, 0),
    (0, 1, 0),
    (0, -1, 0),
    (0, 0, 1),
    (0, 0, -1),
    (1, 1, 0),
    (-1, -1, 0),
    (1, -1, 0),
    (-1, 1, 0),
    (1, 0, 1),
    (-1, 0, -1),
    (1, 0, -1),
    (-1, 0, 1),
    (0, 1, 1),
    (0, -1, -1),
    (0, 1, -1),
    (0, -1, 1),
)
W0, W1, W2 = 1.0 / 3.0, 1.0 / 18.0, 1.0 / 36.0
V0, V1 = 0.25, 0.125
FLOW = 19
POPS = 26
OMEGA_FLOW = 1.6
CONDUCT_RATE = 1.2
SOURCE_RATE = 0.5
HEAT_RATE = 0.1
STEP_SIZE = 0.1

DIRS = ((-1, 0), (1, 0), (0, -1), (0, 1), (-1, -1), (1, -1), (-1, 1), (1, 1))
MESH = pl.DeviceIdType.MESH
PAD = 8


def velocity(pop):
    return VELOCITIES[pop if pop < FLOW else pop - FLOW]


def opposite(pop):
    base = 0 if pop < FLOW else FLOW
    within = pop - base
    if within == 0:
        return pop
    return base + (within + 1 if within % 2 == 1 else within - 1)


def moving(axis, sign):
    return [pop for pop in range(POPS) if velocity(pop)[axis] == sign]


XPOPS = (moving(0, 1), moving(0, -1))
YPOPS = (moving(1, 1), moving(1, -1))


def split3(value):
    high = value.astype(jnp.bfloat16)
    rest = value - high.astype(jnp.float32)
    middle = rest.astype(jnp.bfloat16)
    low = (rest - middle.astype(jnp.float32)).astype(jnp.bfloat16)
    return high, middle, low


def body(
    sizes,
    f_hbm,
    rho_hbm,
    speed_hbm,
    kelvin_hbm,
    obstacle_hbm,
    surface_hbm,
    porosity_hbm,
    patch_hbm,
    holder_hbm,
    out_ref,
    tiles_ref,
    rho_ref,
    speed_ref,
    kelvin_ref,
    obstacle_ref,
    surface_ref,
    porosity_ref,
    patch_ref,
    holder_ref,
    state,
    const,
    acc,
    xsend,
    xrecv,
    ysend,
    yrecv,
    csend,
    crecv,
    yhalo,
    hot,
    label_rows,
    flip_a,
    flip_b,
    column,
    mirror,
    outgoing,
    received,
    load_sem,
    send_sem,
    recv_sem,
    msend_sem,
    mrecv_sem,
    asend_sem,
    arecv_sem,
):
    nx, ny, height, ex, ey, blocks, cap = sizes
    i = lax.axis_index("gx")
    j = lax.axis_index("gy")
    tiles_of = ex // 8

    load = pltpu.make_async_copy(f_hbm, state.at[0, :, :, pl.ds(PAD, ex), :], load_sem.at[8])
    loads = [
        pltpu.make_async_copy(source, target, load_sem.at[n])
        for n, (source, target) in enumerate(
            (
                (rho_hbm, rho_ref),
                (speed_hbm, speed_ref),
                (kelvin_hbm, kelvin_ref),
                (obstacle_hbm, obstacle_ref),
                (surface_hbm, surface_ref),
                (porosity_hbm, porosity_ref),
                (patch_hbm, patch_ref),
                (holder_hbm, holder_ref),
            )
        )
    ]
    load.start()
    for copy in loads:
        copy.start()

    barrier = pltpu.get_barrier_semaphore()

    def inside(di, dj):
        a, b = i + di, j + dj
        return (a >= 0) & (a < nx) & (b >= 0) & (b < ny)

    xrecv[...] = jnp.zeros(xrecv.shape, jnp.float32)
    yrecv[...] = jnp.zeros(yrecv.shape, jnp.float32)
    crecv[...] = jnp.zeros(crecv.shape, jnp.float32)
    acc[...] = jnp.zeros(acc.shape, jnp.float32)

    mirrors = ((nx - 1 - i, j), (i, ny - 1 - j), (nx - 1 - i, ny - 1 - j))
    for dx, dy in DIRS:
        @pl.when(inside(dx, dy))
        def _():
            pl.semaphore_signal(barrier, inc=1, device_id=(i + dx, j + dy), device_id_type=MESH)
    far = max(nx, ny) - 1 > STEPS + 1
    if far:
        for d in range(1, nx):
            target = (lax.rem(i + d, nx), j)
            pl.semaphore_signal(barrier, inc=1, device_id=target, device_id_type=MESH)
        for target in mirrors:
            pl.semaphore_signal(barrier, inc=1, device_id=target, device_id_type=MESH)

    lane = lax.broadcasted_iota(jnp.int32, (8, ey), 1)

    for copy in loads:
        copy.wait()
    for z in range(height):
        fluid = 1.0 - obstacle_ref[z].astype(jnp.float32)
        for axis in range(3):
            const[axis, z] = speed_ref[axis, z] * fluid
        const[3, z] = 4.0 * CONDUCT_RATE * kelvin_ref[z] / rho_ref[z]
        const[4, z] = SOURCE_RATE * surface_ref[z].astype(jnp.float32)
        const[5, z] = fluid

    wide = 1 + (i > 0).astype(jnp.int32) + (i < nx - 1).astype(jnp.int32)
    deep = 1 + (j > 0).astype(jnp.int32) + (j < ny - 1).astype(jnp.int32)
    pl.semaphore_wait(barrier, wide * deep - 1 + (nx - 1 + len(mirrors) if far else 0))
    load.wait()

    def rim_copy(par, k):
        dx, dy = DIRS[k]
        if k < 2:
            src, dst = xsend.at[par, k], xrecv.at[par, k]
        elif k < 4:
            src, dst = ysend.at[par, k - 2], yrecv.at[par, k - 2]
        else:
            src, dst = csend.at[par, k - 4], crecv.at[par, k - 4]
        return pltpu.make_async_remote_copy(
            src_ref=src,
            dst_ref=dst,
            send_sem=send_sem.at[par, k],
            recv_sem=recv_sem.at[par, k],
            device_id=(i + dx, j + dy),
            device_id_type=MESH,
        )

    def send_rim(par):
        for side in range(2):
            for rt in range(tiles_of):
                packed = jnp.zeros((8, ey), jnp.float32)
                for p, pop in enumerate(YPOPS[side]):
                    for z in range(height):
                        q = p * height + z
                        value = state[par, pop, z, PAD + rt * 8 : PAD + rt * 8 + 8, :]
                        shift = q if side == 0 else (q + 1) % ey
                        if shift:
                            value = pltpu.roll(value, shift, 1)
                        packed = jnp.where(lane == q, value, packed)
                ysend[par, side, rt * 8 : rt * 8 + 8, :] = packed
                for k in range(4, 8):
                    dx, dy = DIRS[k]
                    if (0 if dy < 0 else 1) == side:
                        if dx < 0 and rt == 0:
                            csend[par, k - 4] = packed[0:1, :]
                        if dx > 0 and rt == tiles_of - 1:
                            csend[par, k - 4] = packed[7:8, :]
        for k in range(4, 8):
            @pl.when(inside(*DIRS[k]))
            def _():
                rim_copy(par, k).start()
        for k in range(2, 4):
            @pl.when(inside(*DIRS[k]))
            def _():
                rim_copy(par, k).start()
        for side in range(2):
            row = PAD if side == 0 else PAD + ex - 1
            for p, pop in enumerate(XPOPS[side]):
                for z in range(height):
                    q = p * height + z
                    xsend[par, side, q : q + 1, :] = state[par, pop, z, row : row + 1, :]
        for k in range(2):
            @pl.when(inside(*DIRS[k]))
            def _():
                rim_copy(par, k).start()

    def take_rim(par):
        def arrived(k):
            dx, dy = DIRS[k]

            @pl.when(inside(-dx, -dy))
            def _():
                rim_copy(par, k).wait_recv()

        for side in range(2):
            arrived(side)
            row = PAD + ex if side == 0 else PAD - 1
            for p, pop in enumerate(XPOPS[side]):
                for z in range(height):
                    q = p * height + z
                    state[par, pop, z, row : row + 1, :] = xrecv[par, side, q : q + 1, :]
        for side in range(2):
            arrived(2 + side)
            yhalo[side, PAD : PAD + ex, :] = yrecv[par, side]
        for k in range(4, 8):
            arrived(k)
            dx, dy = DIRS[k]
            row = PAD + ex if dx < 0 else PAD - 1
            yhalo[0 if dy < 0 else 1, row : row + 1, :] = crecv[par, k - 4]
        for k in range(8):
            @pl.when(inside(*DIRS[k]))
            def _():
                rim_copy(par, k).wait_send()

    def collide(par, z, rt, put, moments_only=False):
        start = PAD + rt * 8

        def pull(pop):
            cx, cy, cz = velocity(pop)
            zz = z + cz
            if zz < 0 or zz >= height:
                return state[par, opposite(pop), z, start : start + 8, :]
            value = state[par, pop, zz, start + cx : start + cx + 8, :]
            if cy:
                side = 0 if cy == 1 else 1
                q = YPOPS[side].index(pop) * height + zz
                edge = yhalo[side, start + cx : start + cx + 8, :]
                last = ey - 1 if cy == 1 else 0
                shift = (last - q) % ey
                if shift:
                    edge = pltpu.roll(edge, shift, 1)
                value = pltpu.roll(value, (-cy) % ey, 1)
                value = jnp.where(lane == last, edge, value)
            return value

        rows = slice(rt * 8, rt * 8 + 8)
        ux, uy, uz = const[0, z, rows, :], const[1, z, rows, :], const[2, z, rows, :]
        coupling = const[3, z, rows, :]
        source = const[4, z, rows, :]
        fluid = const[5, z, rows, :] > 0.5

        b = [pull(FLOW + k) for k in range(7)]
        tsum = V0 * b[0] + V1 * ((b[1] + b[2]) + (b[3] + b[4]) + (b[5] + b[6]))
        qx, qy, qz = V1 * (b[1] - b[2]), V1 * (b[3] - b[4]), V1 * (b[5] - b[6])
        qu = qx * ux + qy * uy + qz * uz
        warm = CONDUCT_RATE * (tsum + 4.0 * qu) + source
        if not moments_only:
            for k in range(7):
                put(FLOW + k, z, rt, (1.0 - CONDUCT_RATE) * b[k] + warm)

        a = [None if moments_only and k == 0 else pull(k) for k in range(FLOW)]
        sm = {k: a[k] + a[k + 1] for k in range(1, FLOW, 2)}
        df = {k: a[k] - a[k + 1] for k in range(1, FLOW, 2)}
        sx = (3.0 * W1) * df[1] + (3.0 * W2) * ((df[7] + df[9]) + (df[11] + df[13]))
        sy = (3.0 * W1) * df[3] + (3.0 * W2) * ((df[7] - df[9]) + (df[15] + df[17]))
        sz = (3.0 * W1) * df[5] + (3.0 * W2) * ((df[11] - df[13]) + (df[15] - df[17]))
        sens = HEAT_RATE * tsum - rho_ref[z, rows, :] * (ux * sx + uy * sy + uz * sz)
        if moments_only:
            return sens
        xy, xz, yz = sm[7] + sm[9], sm[11] + sm[13], sm[15] + sm[17]
        mass = W0 * a[0] + W1 * (sm[1] + sm[3] + sm[5]) + W2 * (xy + xz + yz)
        quad = (
            (ux * ux) * (W1 * sm[1] + W2 * (xy + xz))
            + (uy * uy) * (W1 * sm[3] + W2 * (xy + yz))
            + (uz * uz) * (W1 * sm[5] + W2 * (xz + yz))
            + (2.0 * W2)
            * (
                (ux * uy) * (sm[7] - sm[9])
                + (ux * uz) * (sm[11] - sm[13])
                + (uy * uz) * (sm[15] - sm[17])
            )
        )
        square = ux * ux + uy * uy + uz * uz
        scalar = mass * (1.0 - 1.5 * square) + 4.5 * quad
        base = OMEGA_FLOW * scalar - coupling * qu
        gx = OMEGA_FLOW * sx + coupling * qx
        gy = OMEGA_FLOW * sy + coupling * qy
        gz = OMEGA_FLOW * sz + coupling * qz
        along = {
            1: gx,
            3: gy,
            5: gz,
            7: gx + gy,
            9: gx - gy,
            11: gx + gz,
            13: gx - gz,
            15: gy + gz,
            17: gy - gz,
        }
        keep = 1.0 - OMEGA_FLOW

        put(0, z, rt, jnp.where(fluid, keep * a[0] + base, a[0]))
        for k in range(1, FLOW, 2):
            put(k, z, rt, jnp.where(fluid, keep * a[k] + (base + along[k]), a[k + 1]))
            put(k + 1, z, rt, jnp.where(fluid, keep * a[k + 1] + (base - along[k]), a[k]))
        return sens

    send_rim(0)

    number = lax.broadcasted_iota(jnp.int32, (blocks, ey), 0)
    below = (
        lax.broadcasted_iota(jnp.int32, (ey, ey), 0) < lax.broadcasted_iota(jnp.int32, (ey, ey), 1)
    ).astype(jnp.bfloat16)
    place = lax.broadcasted_iota(jnp.int32, (TILE, ey), 0).astype(jnp.float32)
    running = jnp.zeros((blocks, 1), jnp.float32)
    for x in range(ex):
        hits = (patch_ref[x : x + 1, :] == number).astype(jnp.float32)
        earlier = jnp.dot(
            hits.astype(jnp.bfloat16), below, preferred_element_type=jnp.float32
        )
        rank = jnp.sum(hits * (earlier + running), axis=0, keepdims=True)
        running = running + jnp.sum(hits, axis=1, keepdims=True)
        hot[:, x * ey : (x + 1) * ey] = (place == rank).astype(jnp.bfloat16)
        label_rows[:, x * ey : (x + 1) * ey] = hits

    def gathered(field):
        columns = jnp.concatenate(
            [
                label_rows[:, x * ey : (x + 1) * ey] * field[x : x + 1, :]
                for x in range(ex)
            ],
            axis=1,
        )
        parts = jnp.concatenate(split3(columns), axis=0)
        result = lax.dot_general(
            parts, hot[...], (((1,), (1,)), ((), ())), preferred_element_type=jnp.float32
        )
        return result[:blocks] + result[blocks : 2 * blocks] + result[2 * blocks :]

    design = gathered(porosity_ref[...])

    owner_row = jnp.concatenate(
        [
            holder_ref[...].astype(jnp.float32),
            jnp.zeros((1, TILE - blocks), jnp.float32),
        ],
        axis=1,
    )
    rows_of = lax.broadcasted_iota(jnp.int32, (blocks, TILE), 0)
    lanes_of = lax.broadcasted_iota(jnp.int32, (blocks, TILE), 1)
    diagonal = (rows_of == lanes_of).astype(jnp.float32)
    owner = jnp.sum(owner_row * diagonal, axis=1, keepdims=True)
    same = ((owner == owner_row) & (rows_of < lanes_of) & (lanes_of < blocks)).astype(jnp.float32)
    rank_row = jnp.sum(same, axis=0, keepdims=True)
    slot_row = owner_row * float(cap) + rank_row
    slots = nx * cap
    choose = (
        (lax.broadcasted_iota(jnp.int32, (slots, TILE), 0).astype(jnp.float32) == slot_row)
        & (lax.broadcasted_iota(jnp.int32, (slots, TILE), 1) < blocks)
    ).astype(jnp.bfloat16)

    def step(s, carry):
        par = lax.rem(s, 2)

        def put(pop, z, rt, value):
            start = PAD + rt * 8
            state[1 - par, pop, z, start : start + 8, :] = value

        take_rim(par)
        for rt in range(tiles_of):
            sens = collide(par, 0, rt, put)
            for z in range(1, height):
                sens = sens + collide(par, z, rt, put)
            acc[rt * 8 : rt * 8 + 8, :] += sens
        send_rim(1 - par)
        return carry

    lax.fori_loop(0, STEPS - 1, step, 0)

    last = (STEPS - 1) % 2

    def put_out(pop, z, rt, value):
        out_ref[pop, z, rt * 8 : rt * 8 + 8, :] = value

    take_rim(last)
    for rt in range(tiles_of):
        sens = collide(last, 0, rt, None, True)
        for z in range(1, height):
            sens = sens + collide(last, z, rt, None, True)
        column[rt * 8 : rt * 8 + 8, :] = acc[rt * 8 : rt * 8 + 8, :] + sens

    def mirror_copy(m):
        return pltpu.make_async_remote_copy(
            src_ref=column,
            dst_ref=mirror.at[m],
            send_sem=msend_sem.at[m],
            recv_sem=mrecv_sem.at[m],
            device_id=mirrors[m],
            device_id_type=MESH,
        )

    for m in (2, 1, 0):
        mirror_copy(m).start()
    for rt in range(tiles_of):
        for z in range(height):
            collide(last, z, rt, put_out)
    for m in range(3):
        mirror_copy(m).wait()
    for x in range(ex):
        flip_a[x : x + 1, :] = mirror[0, ex - 1 - x : ex - x, :]
        flip_b[x : x + 1, :] = mirror[2, ex - 1 - x : ex - x, :]
    reverse = (
        lax.broadcasted_iota(jnp.int32, (ey, ey), 0) + lax.broadcasted_iota(jnp.int32, (ey, ey), 1)
        == ey - 1
    ).astype(jnp.bfloat16)
    turned = jnp.dot(
        jnp.concatenate(split3(mirror[1] + flip_b[...]), axis=0),
        reverse,
        preferred_element_type=jnp.float32,
    )
    symmetric = (
        column[...] + flip_a[...] + (turned[:ex] + turned[ex : 2 * ex] + turned[2 * ex :])
    )
    sens = gathered(symmetric)
    spread = jnp.sqrt(jnp.mean(sens * sens, axis=1, keepdims=True) + 1e-06)
    fresh = jnp.clip(design - STEP_SIZE * sens / spread, 0.0, 1.0)
    padded = jnp.concatenate([fresh, jnp.zeros((TILE - blocks, TILE), jnp.float32)], axis=0)
    parts = jnp.concatenate(split3(padded), axis=1)
    sent = jnp.dot(choose, parts, preferred_element_type=jnp.float32)
    sent = sent[:, :TILE] + sent[:, TILE : 2 * TILE] + sent[:, 2 * TILE :]
    for o in range(nx):
        outgoing[o] = sent[o * cap : (o + 1) * cap, :]

    def owner_copy(d):
        target = lax.rem(i + d, nx)
        return pltpu.make_async_remote_copy(
            src_ref=outgoing.at[target],
            dst_ref=received.at[i],
            send_sem=asend_sem.at[d],
            recv_sem=arecv_sem.at[d],
            device_id=(target, j),
            device_id_type=MESH,
        )

    def arriving(d):
        origin = lax.rem(i + nx - d, nx)
        return pltpu.make_async_remote_copy(
            src_ref=outgoing.at[origin],
            dst_ref=received.at[origin],
            send_sem=asend_sem.at[d],
            recv_sem=arecv_sem.at[d],
            device_id=(origin, j),
            device_id_type=MESH,
        )

    for d in range(1, nx):
        owner_copy(d).start()
    received[i] = outgoing[i]
    for d in range(1, nx):
        owner_copy(d).wait_send()
        arriving(d).wait_recv()
    for o in range(nx):
        tiles_ref[o * cap : (o + 1) * cap, :] = received[o]


def on_device(
    dual_distributions,
    primal_fluid_rho,
    forward_flow_speed,
    primal_kelvin_values,
    obstacle_mask,
    objective_surface_mask,
    pillar_porosity,
    pillar_design_patch,
    patch_holder,
):
    nx, ny = lax.axis_size("gx"), lax.axis_size("gy")
    pops, height, ex, ey = dual_distributions.shape
    blocks = ex * ey // TILE
    cap = max(2, 2 * blocks // nx)
    nxp, nyp = len(XPOPS[0]), len(YPOPS[0])
    f32 = jnp.float32
    vmem = pl.BlockSpec(memory_space=pltpu.VMEM)
    hbm = pl.BlockSpec(memory_space=pl.ANY)
    return pl.pallas_call(
        functools.partial(body, (nx, ny, height, ex, ey, blocks, cap)),
        out_shape=(
            pltpu.VMEM(dual_distributions.shape, f32),
            pltpu.VMEM((nx * cap, TILE), f32),
        ),
        in_specs=[hbm] * 9,
        out_specs=(vmem, vmem),
        scratch_shapes=[
            pltpu.VMEM(primal_fluid_rho.shape, f32),
            pltpu.VMEM(forward_flow_speed.shape, f32),
            pltpu.VMEM(primal_kelvin_values.shape, f32),
            pltpu.VMEM(obstacle_mask.shape, jnp.int32),
            pltpu.VMEM(objective_surface_mask.shape, jnp.int32),
            pltpu.VMEM(pillar_porosity.shape, f32),
            pltpu.VMEM(pillar_design_patch.shape, jnp.int32),
            pltpu.VMEM((1, blocks), jnp.int32),
            pltpu.VMEM((2, pops, height, ex + 2 * PAD, ey), f32),
            pltpu.VMEM((6, height, ex, ey), f32),
            pltpu.VMEM((ex, ey), f32),
            pltpu.VMEM((2, 2, nxp * height, ey), f32),
            pltpu.VMEM((2, 2, nxp * height, ey), f32),
            pltpu.VMEM((2, 2, ex, ey), f32),
            pltpu.VMEM((2, 2, ex, ey), f32),
            pltpu.VMEM((2, 4, 1, ey), f32),
            pltpu.VMEM((2, 4, 1, ey), f32),
            pltpu.VMEM((2, ex + 2 * PAD, ey), f32),
            pltpu.VMEM((TILE, ex * ey), jnp.bfloat16),
            pltpu.VMEM((blocks, ex * ey), f32),
            pltpu.VMEM((ex, ey), f32),
            pltpu.VMEM((ex, ey), f32),
            pltpu.VMEM((ex, ey), f32),
            pltpu.VMEM((3, ex, ey), f32),
            pltpu.VMEM((nx, cap, TILE), f32),
            pltpu.VMEM((nx, cap, TILE), f32),
            pltpu.SemaphoreType.DMA((9,)),
            pltpu.SemaphoreType.DMA((2, 8)),
            pltpu.SemaphoreType.DMA((2, 8)),
            pltpu.SemaphoreType.DMA((3,)),
            pltpu.SemaphoreType.DMA((3,)),
            pltpu.SemaphoreType.DMA((nx,)),
            pltpu.SemaphoreType.DMA((nx,)),
        ],
        compiler_params=pltpu.CompilerParams(collective_id=0, has_side_effects=True),
    )(
        dual_distributions,
        primal_fluid_rho,
        forward_flow_speed,
        primal_kelvin_values,
        obstacle_mask,
        objective_surface_mask,
        pillar_porosity,
        pillar_design_patch,
        patch_holder.T,
    )


def solution(mesh):
    in_specs = (
        P(None, None, "gx", "gy"),
        P(None, "gx", "gy"),
        P(None, None, "gx", "gy"),
        P(None, "gx", "gy"),
        P(None, "gx", "gy"),
        P(None, "gx", "gy"),
        P("gx", "gy"),
        P("gx", "gy"),
        P(("gx", "gy"), None),
    )
    out_specs = (P(None, None, "gx", "gy"), P(("gx", "gy"), None))
    return jax.shard_map(
        on_device, mesh=mesh, in_specs=in_specs, out_specs=out_specs, check_vma=False
    )
```
